256 devices in a mesh: space: 32 (over y, x, core), wave: 8 (over z).
Axes of the slice: x: 4, y: 4, z: 8, core: 2. Of those that a mesh axis runs over, the one named last changes fastest.
Arguments:
- noise: float32 [8, 3, 32768], P(None, None, 'space'), may hold values from -6 to 6
- positions: float32 [3, 32768], P(None, 'space'), may hold values from 0 to 32, as said below
- wave_index: int32 [3, 4096], P(None, 'wave'), may hold values from -16 to 16, as said below
- tile_lists: int32 [256, 8], P('space'), may hold values from 0 to 23, as said below
- tile_counts: int32 [256], P('space'), may hold values from 0 to 8, as said below
Outputs:
- displacement: float32 [8, 3, 32768], P(None, None, 'space')
The draws below stay inside these ranges and needn't reach their ends.
Inputs may be any that keep to these rules, and one draw needn't show every extreme that they name: `positions`: particle j has x between j // 1024 and j // 1024 + 1, and y and z between 0 and 8. `wave_index`: row 0 holds n_1 from 1 to 16; rows 1 and 2 hold values from -16 to 15. `tile_lists`: A tile's 8 entries are distinct; window indices below 8 name tiles of the slab before, the next 8 tiles of the own slab, the rest tiles of the slab after. `tile_counts`: the counts of the 8 tiles of one slab add up to exactly 32, and in every slab one tile has 8.
All inputs are finite; a program needn't handle non-finite values.
Results may differ from the reference program's by a relative error of at most 0.0003.
Values sent between devices are 32-bit elements; how exact they have to be, the bound alone decides.
A program may use at most 64 MiB of HBM per device.

```python
import math
import jax
import jax.numpy as jnp
from jax import lax

NVEC = 8
P_BLK = 1024
TILE = 128
KW = 4096
NB_MOST = 8
DEGREE = 3
TILES = 8
TILES_ALL = 256
PAIR_MOST = 32
PARTICLES = 32768
N_SPACE = 32


def draw_positions(key, part):
    across = jax.random.uniform(jax.random.fold_in(key, 11), (PARTICLES,), jnp.float32)
    cross = jax.random.uniform(jax.random.fold_in(key, 12), (2, PARTICLES), jnp.float32)
    slab_start = (jnp.arange(PARTICLES) // P_BLK).astype(jnp.float32)
    return jnp.concatenate([(slab_start + across)[None, :], 8.0 * cross], axis=0).astype(jnp.float32)


def draw_wave_index(key, part):
    first_row = jax.random.randint(jax.random.fold_in(key, 21), (1, KW), 1, 17)
    other_rows = jax.random.randint(jax.random.fold_in(key, 22), (2, KW), -16, 16)
    return jnp.concatenate([first_row, other_rows], axis=0).astype(jnp.int32)


def draw_tile_lists(key, part):
    subkeys = jax.random.split(jax.random.fold_in(key, 31), TILES_ALL)

    def pick_window(subkey):
        return jax.random.permutation(subkey, 3 * TILES)[:NB_MOST]
    return jax.vmap(pick_window)(subkeys).astype(jnp.int32)


def draw_tile_counts(key, part):
    subkeys = jax.random.split(jax.random.fold_in(key, 41), TILES_ALL // TILES)

    def block_counts(subkey):
        full_tile = jax.random.randint(jax.random.fold_in(subkey, 1), (), 0, TILES)
        chosen = jax.random.permutation(jax.random.fold_in(subkey, 2), (TILES - 1) * NB_MOST)[:PAIR_MOST - NB_MOST]
        owner = chosen // NB_MOST
        others = jnp.sum((owner[:, None] == jnp.arange(TILES - 1)[None, :]).astype(jnp.int32), axis=0)
        index_ids = jnp.arange(TILES)
        shifted = jnp.clip(index_ids - (index_ids > full_tile).astype(jnp.int32), 0, TILES - 2)
        return jnp.where(index_ids == full_tile, NB_MOST, others[shifted]).astype(jnp.int32)
    return jax.vmap(block_counts)(subkeys).reshape(TILES_ALL).astype(jnp.int32)


def levels(key, shape, cuts, smallest, top_value):
    level = 1.0
    for axis_at, shards_of in cuts:
        heights = jax.random.uniform(jax.random.fold_in(jax.random.fold_in(key, 6), axis_at), (shards_of,), jnp.float32, smallest / len(cuts), top_value / len(cuts))
        level = level * jnp.repeat(jnp.exp(heights), shape[axis_at] // shards_of).reshape((-1,) + (1,) * (len(shape) - 1 - axis_at))
    return level


def scatter_about(own_key, shape, spread, reach, cuts=(), kind=jnp.bfloat16):
    values = jax.random.normal(own_key, shape, jnp.float32) * spread
    if len(cuts) > 0:
        values = levels(own_key, shape, cuts, -0.22, 0.18) * values
    return jnp.clip(values, min=-reach, max=reach).astype(kind)


def setup_inputs(seed: int = 0) -> dict:
    splits = jax.random.split(jax.random.key(seed), 6)
    return {
        "noise": scatter_about(splits[0], (NVEC, 3, PARTICLES), 1.0, 6.0, ((2, 32),), jnp.float32),
        "positions": draw_positions(jax.random.fold_in(splits[5], 71), 0),
        "wave_index": draw_wave_index(jax.random.fold_in(splits[5], 71), 0),
        "tile_lists": draw_tile_lists(jax.random.fold_in(splits[5], 71), 0),
        "tile_counts": draw_tile_counts(jax.random.fold_in(splits[5], 71), 0),
    }


PRECISE = lax.Precision.HIGHEST
SIDE_CROSS = 8.0
NEAR_SQUARE = 0.36
NEAR_AMP = 0.15
FAR_AMP = 8.0
SPLIT_SQUARE = 64.0
SCREEN = 4.0
SAFETY = 1.25
SPREAD = 100.0
EPSILON = 1e-06

def pair_block(target, source, self_flag, live_weight, length_x):
    box_sides = jnp.array([length_x, SIDE_CROSS, SIDE_CROSS], jnp.float32)[:, None, None]
    offset = target[:, None, :] - source[:, :, None]
    offset = offset - box_sides * jnp.floor(offset / box_sides + 0.5)
    distance_sq = lax.optimization_barrier(jnp.sum(offset * offset, axis=0))
    tile_width = target.shape[1]
    diagonal_mask = jnp.arange(tile_width)[:, None] == jnp.arange(tile_width)[None, :]
    keep_mask = jnp.where(diagonal_mask & self_flag, 0.0, 1.0) * live_weight
    envelope = NEAR_AMP * jnp.exp(-distance_sq / NEAR_SQUARE) * keep_mask
    outer_product = offset[None, :, :, :] * offset[:, None, :, :]
    identity = jnp.eye(3, dtype=jnp.float32)[:, :, None, None]
    pair_matrix = (identity + outer_product / NEAR_SQUARE) * envelope[None, None]
    return jnp.transpose(pair_matrix, (0, 2, 1, 3)).reshape(3 * tile_width, 3 * tile_width)

def wave_terms(indices, length_x):
    box_sides = jnp.array([length_x, SIDE_CROSS, SIDE_CROSS], jnp.float32)[:, None]
    wave_vectors = 2.0 * math.pi * indices.astype(jnp.float32) / box_sides
    wave_square = lax.optimization_barrier(jnp.sum(wave_vectors * wave_vectors, axis=0))
    scaled_square = wave_square / SPLIT_SQUARE
    weight = FAR_AMP * (1.0 + scaled_square) * jnp.exp(-scaled_square) / (KW * (wave_square + SCREEN))
    unit_waves = wave_vectors / jnp.sqrt(wave_square)
    return (wave_vectors, weight, unit_waves)

def make_phases(positions, wave_vectors):
    phase_angles = positions[0][:, None] * wave_vectors[0][None, :] + positions[1][:, None] * wave_vectors[1][None, :] + positions[2][:, None] * wave_vectors[2][None, :]
    return jnp.concatenate([jnp.cos(phase_angles), jnp.sin(phase_angles)], axis=1)

def project(factors, weight, unit_waves):
    along_wave = lax.optimization_barrier(jnp.sum(factors * unit_waves[None, :, None, :], axis=1))
    return weight * (factors - unit_waves[None, :, None, :] * along_wave[:, None])

def far_apply(forces, positions, wave_index):
    vectors = forces.shape[0]
    row_count = vectors * 3
    flattened = forces.reshape(row_count, forces.shape[2])
    wave_blocks = jnp.transpose(wave_index.reshape(3, KW // 512, 512), (1, 0, 2))

    def add_block(running_sum, indices):
        wave_vectors, weight, unit_waves = wave_terms(indices, float(N_SPACE))
        phases = make_phases(positions, wave_vectors)
        factors = jnp.dot(flattened, phases, precision=PRECISE, preferred_element_type=jnp.float32).reshape(vectors, 3, 2, 512)
        weighted = project(factors, weight, unit_waves).reshape(row_count, 1024)
        back = lax.dot_general(weighted, phases, (((1,), (1,)), ((), ())), precision=PRECISE, preferred_element_type=jnp.float32)
        return (running_sum + back, None)
    running_sum, _ = lax.scan(add_block, jnp.zeros((row_count, forces.shape[2]), jnp.float32), wave_blocks)
    return running_sum.reshape(forces.shape)

def near_apply(forces, positions, tile_lists, tile_counts):
    vectors = forces.shape[0]

    def one_tile(tile_id):
        slab_id = tile_id // TILES
        own_tile = tile_id % TILES
        target = lax.dynamic_slice_in_dim(positions, (tile_id * TILE).astype(jnp.int32), TILE, 1)

        def one_slot(slot_id):
            window = tile_lists[tile_id, slot_id]
            source_tile = ((slab_id - 1 + window // TILES) % N_SPACE * TILES + window % TILES).astype(jnp.int32)
            source = lax.dynamic_slice_in_dim(positions, source_tile * TILE, TILE, 1)
            pushed = lax.dynamic_slice_in_dim(forces, source_tile * TILE, TILE, 2).reshape(vectors, 3 * TILE)
            live_weight = jnp.where(slot_id < tile_counts[tile_id], 1.0, 0.0)
            matrix = pair_block(target, source, window == TILES + own_tile, live_weight, float(N_SPACE))
            return jnp.dot(pushed, matrix, precision=PRECISE, preferred_element_type=jnp.float32)
        slot_parts = jax.vmap(one_slot)(jnp.arange(NB_MOST, dtype=jnp.int32))
        return lax.optimization_barrier(jnp.sum(slot_parts, axis=0)).reshape(vectors, 3, TILE)
    pieces = lax.map(one_tile, jnp.arange(TILES_ALL, dtype=jnp.int32))
    return jnp.transpose(pieces, (1, 2, 0, 3)).reshape(forces.shape)

def chebyshev(lower_bound, upper_bound):
    node_count = DEGREE + 1
    node_angles = (jnp.arange(node_count, dtype=jnp.float32) + 0.5) * (math.pi / node_count)
    samples = jnp.sqrt(0.5 * (upper_bound - lower_bound) * jnp.cos(node_angles) + 0.5 * (upper_bound + lower_bound))
    orders = jnp.arange(node_count, dtype=jnp.float32)
    coeffs = 2.0 / node_count * lax.optimization_barrier(jnp.sum(samples[None, :] * jnp.cos(orders[:, None] * node_angles[None, :]), axis=1))
    return coeffs * jnp.where(orders == 0.0, 0.5, 1.0)

def reference(noise, positions, wave_index, tile_lists, tile_counts):

    def mobility(forces):
        return forces + near_apply(forces, positions, tile_lists, tile_counts) + far_apply(forces, positions, wave_index)
    first_image = mobility(noise)
    second = mobility(first_image)
    ratios = lax.optimization_barrier(jnp.sum(second * second, axis=(1, 2))) / (lax.optimization_barrier(jnp.sum(first_image * first_image, axis=(1, 2))) + EPSILON)
    upper_bound = SAFETY * jnp.sqrt(jnp.max(ratios))
    lower_bound = upper_bound / SPREAD
    coeffs = chebyshev(lower_bound, upper_bound)
    bound_sum = upper_bound + lower_bound
    bound_span = upper_bound - lower_bound
    previous = noise
    current = (2.0 * first_image - bound_sum * noise) / bound_span
    mapped = (2.0 * second - bound_sum * first_image) / bound_span
    running_sum = coeffs[0] * previous + coeffs[1] * current
    for degree_step in range(2, DEGREE + 1):
        following = 2.0 * (2.0 * mapped - bound_sum * current) / bound_span - previous
        running_sum = running_sum + coeffs[degree_step] * following
        if degree_step < DEGREE:
            mapped = mobility(following)
        previous, current = (current, following)
    return running_sum
```

```python
import functools
import math

import jax
import jax.numpy as jnp
from jax import lax
from jax.experimental import pallas as pl
from jax.experimental.pallas import tpu as pltpu
from jax.sharding import PartitionSpec as P

MESH = pl.DeviceIdType.MESH
F32 = jnp.float32
BF16 = jnp.bfloat16

KW = 4096
DEGREE = 3
TILE = 128
SIDE_CROSS = 8.0
NEAR_SQUARE = 0.36
NEAR_AMP = 0.15
FAR_AMP = 8.0
SPLIT_SQUARE = 64.0
SCREEN = 4.0
SAFETY = 1.25
SPREAD = 100.0
EPSILON = 1e-06

SINE = (6.283185160087367, -41.34165503087954, 81.60100403735636, -76.54978142115317, 39.5366991046531)


def split_rows(x):
    high = x.astype(BF16).astype(F32)
    return jnp.concatenate([high, x - high], axis=0).astype(BF16)


def sine_of_turns(a):
    a2 = a * a
    p = F32(SINE[-1])
    for c in SINE[-2::-1]:
        p = p * a2 + F32(c)
    return p * a


def nearest(x):
    return jnp.floor(x + 0.5)


def kernel(
    n_space,
    n_wave,
    noise_ref,
    pos_ref,
    wave_ref,
    lists_ref,
    counts_ref,
    out_ref,
    ph_hi,
    ph_lo,
    posw,
    ev,
    nf,
    bm_hi,
    bm_lo,
    u,
    near,
    sbuf,
    rs,
    agb,
    vbuf,
    wr,
    nsrc,
    nrecv,
    outb,
    rs_s,
    rs_r,
    ag_s,
    ag_r,
    wr_s,
    wr_r,
    wa_s,
    wa_r,
    halo_s,
    halo_r,
    pos_s,
    pos_r,
    norm_s,
    norm_r,
):
    me = lax.axis_index("space")
    wv = lax.axis_index("wave")
    up = lax.rem(me + 1, n_space)
    down = lax.rem(me + n_space - 1, n_space)
    tiles = n_wave

    barrier = pltpu.get_barrier_semaphore()

    def greet_space(d, _):
        pl.semaphore_signal(
            barrier, inc=1, device_id=(lax.rem(me + d, n_space), wv), device_id_type=MESH
        )
        return 0

    def greet_wave(d, _):
        pl.semaphore_signal(
            barrier, inc=1, device_id=(me, lax.rem(wv + d, n_wave)), device_id_type=MESH
        )
        return 0

    lax.fori_loop(1, n_space, greet_space, 0)
    lax.fori_loop(1, n_wave, greet_wave, 0)

    def remote(src, dst, ssem, rsem, s, w):
        return pltpu.make_async_remote_copy(
            src_ref=src,
            dst_ref=dst,
            send_sem=ssem,
            recv_sem=rsem,
            device_id=(s, w),
            device_id_type=MESH,
        )

    for t in range(tiles):
        lanes = slice(t * TILE, (t + 1) * TILE)
        posw[tiles + t] = jnp.concatenate(
            [pos_ref[:, lanes], jnp.zeros((5, TILE), F32)], axis=0
        )
        u[0, tiles + t] = noise_ref[:, lanes]

    waves = wave_ref.shape[1]
    n_all = wave_ref[...].astype(F32)
    n_rows = [jnp.broadcast_to(n_all[c : c + 1], (8, waves)) for c in range(3)]
    ka = n_rows[0] * F32(2.0 * math.pi / n_space)
    kb = n_rows[1] * F32(2.0 * math.pi / SIDE_CROSS)
    kc = n_rows[2] * F32(2.0 * math.pi / SIDE_CROSS)
    plane = ka * ka + kb * kb
    square = plane + kc * kc
    scaled = square / SPLIT_SQUARE
    weight = FAR_AMP * (1.0 + scaled) * jnp.exp(-scaled) / (KW * (square + SCREEN))
    root = jnp.sqrt(weight)
    rho = jnp.sqrt(plane)
    length = jnp.sqrt(square)
    ev[0] = -root * kb / rho
    ev[1] = root * ka / rho
    ev[2] = -root * ka * kc / (rho * length)
    ev[3] = -root * kb * kc / (rho * length)
    ev[4] = root * rho / length
    for c in range(3):
        nf[c] = n_rows[c]

    def make_phases(t, _):
        cols = jnp.transpose(posw[tiles + t])
        for j in range(TILE // 16):
            rows = pl.ds(pl.multiple_of(t * TILE + j * 16, 16), 16)
            part = cols[j * 16 : (j + 1) * 16]
            tx = part[:, 0:1] * F32(1.0 / n_space)
            ty = part[:, 1:2] * F32(1.0 / SIDE_CROSS)
            tz = part[:, 2:3] * F32(1.0 / SIDE_CROSS)
            turns = tx * nf[0, 0:1] + ty * nf[1, 0:1] + tz * nf[2, 0:1]
            r = turns - nearest(turns)
            q = r - 0.25
            q = q - nearest(q)
            cosine = sine_of_turns(0.25 - jnp.abs(r))
            sine = sine_of_turns(0.25 - jnp.abs(q))
            for at, value in ((0, cosine), (waves, sine)):
                high = value.astype(BF16)
                ph_hi[rows, at : at + waves] = high
                ph_lo[rows, at : at + waves] = (value - high.astype(F32)).astype(BF16)
        return 0

    lax.fori_loop(0, tiles, make_phases, 0)

    def halo(k):
        own = u.at[k, pl.ds(tiles, tiles)]
        return (
            remote(own, u.at[k, pl.ds(0, tiles)], halo_s.at[k, 0], halo_r.at[k, 0], up, wv),
            remote(own, u.at[k, pl.ds(2 * tiles, tiles)], halo_s.at[k, 1], halo_r.at[k, 1], down, wv),
        )

    own_pos = posw.at[pl.ds(tiles, tiles)]
    pos_copies = (
        remote(own_pos, posw.at[pl.ds(0, tiles)], pos_s.at[0], pos_r.at[0], up, wv),
        remote(own_pos, posw.at[pl.ds(2 * tiles, tiles)], pos_s.at[1], pos_r.at[1], down, wv),
    )

    pl.semaphore_wait(barrier, n_space - 1 + n_wave - 1)

    for copy in pos_copies + halo(0):
        copy.start()

    def pair_of(i):
        j = wv * (32 // n_wave) + i
        total = jnp.int32(0)
        tile = jnp.int32(0)
        base = jnp.int32(0)
        for t in range(tiles):
            total = total + counts_ref[t]
            past = total <= j
            tile = tile + past.astype(jnp.int32)
            base = jnp.where(past, total, base)
        tile = jnp.minimum(tile, tiles - 1)
        slot = jnp.clip(j - base, 0, lists_ref.shape[1] - 1)
        return tile, jnp.clip(lists_ref[tile, slot], 0, 3 * tiles - 1)

    pairs = 32 // n_wave

    def build_pair(i, _):
        tile, source = pair_of(i)
        target_rows = posw[tiles + tile]
        source_cols = jnp.transpose(posw[source])
        offs = []
        for c, side in enumerate((float(n_space), SIDE_CROSS, SIDE_CROSS)):
            off = target_rows[c : c + 1] - source_cols[:, c : c + 1]
            offs.append(off - F32(side) * jnp.floor(off * F32(1.0 / side) + 0.5))
        square = offs[0] * offs[0] + offs[1] * offs[1] + offs[2] * offs[2]
        diagonal = lax.broadcasted_iota(jnp.int32, (TILE, TILE), 0) == lax.broadcasted_iota(
            jnp.int32, (TILE, TILE), 1
        )
        own = jnp.where(source == tiles + tile, F32(0.0), F32(1.0))
        keep = jnp.where(diagonal, own, F32(1.0))
        envelope = NEAR_AMP * jnp.exp(-square / NEAR_SQUARE) * keep
        scaled_env = envelope / NEAR_SQUARE
        for a in range(3):
            left = offs[a] * scaled_env
            for b in range(a, 3):
                block = left * offs[b]
                if a == b:
                    block = block + envelope
                high = block.astype(BF16)
                low = (block - high.astype(F32)).astype(BF16)
                for p, q in sorted({(a, b), (b, a)}):
                    at = (i, slice(p * TILE, (p + 1) * TILE), slice(q * TILE, (q + 1) * TILE))
                    bm_hi[at] = high
                    bm_lo[at] = low
        return 0

    def near_apply(k):
        near[...] = jnp.zeros_like(near)

        def one_pair(i, _):
            tile, source = pair_of(i)
            f = u[k, source]
            lhs = split_rows(jnp.concatenate([f[0:8], f[8:16], f[16:24]], axis=1))
            res = jnp.dot(lhs, bm_hi[i], preferred_element_type=F32) + jnp.dot(
                lhs, bm_lo[i], preferred_element_type=F32
            )
            res = res[0:8] + res[8:16]
            res = jnp.concatenate([res[:, c * TILE : (c + 1) * TILE] for c in range(3)], axis=0)
            for t in range(tiles):
                near[t] += jnp.where(tile == t, res, 0.0)
            return 0

        lax.fori_loop(0, pairs, one_pair, 0)

    def send_space(src_of, dst, ssem, rsem):
        def one(d, _):
            peer = lax.rem(me + d, n_space)
            remote(src_of(peer), dst, ssem, rsem, peer, wv).start()
            return 0

        lax.fori_loop(1, n_space, one, 0)

    def all_but_one(ref, count, ssem, rsem):
        some = ref.at[pl.ds(0, count)]
        return remote(some, some, ssem, rsem, up, wv)

    waiting = []
    sent = []

    for k in range(DEGREE):
        x = jnp.concatenate([u[k, tiles + t] for t in range(tiles)], axis=1)
        lhs = split_rows(x)
        step = 256
        for n in range(waves // step):
            parts = []
            for half in range(2):
                cols = slice(half * waves + n * step, half * waves + (n + 1) * step)
                c = jnp.dot(lhs, ph_hi[:, cols], preferred_element_type=F32) + jnp.dot(
                    lhs, ph_lo[:, cols], preferred_element_type=F32
                )
                parts.append(c[0:24] + c[24:48])
            for half in range(2):
                c = parts[half]
                for q in range(step // TILE):
                    lanes = slice(q * TILE, (q + 1) * TILE)
                    at = slice(n * step + q * TILE, n * step + (q + 1) * TILE)
                    c0, c1, c2 = c[0:8, lanes], c[8:16, lanes], c[16:24, lanes]
                    d0 = ev[0, :, at] * c0 + ev[1, :, at] * c1
                    d1 = ev[2, :, at] * c0 + ev[3, :, at] * c1 + ev[4, :, at] * c2
                    chip = half * (waves // TILE) + n * (step // TILE) + q
                    for tangent, d in ((0, d0), (1, d1)):
                        slot = 2 * (tangent * (2 * waves // TILE) + chip)
                        sbuf[k, slot] = d[0:4]
                        sbuf[k, slot + 1] = d[4:8]
        rs[k, me] = sbuf[k, me]
        send_space(lambda peer: sbuf.at[k, peer], rs.at[k, me], rs_s.at[k], rs_r.at[k])
        sent.append((sbuf.at[k], n_space - 1, rs_s.at[k], rs_r.at[k]))

        if k > 0:
            total = jnp.zeros((8, TILE), F32)
            for t in range(tiles):
                v = u[k, tiles + t]
                v = v * v
                total = total + (v[0:8] + v[8:16] + v[16:24])
            lane_sum = jnp.sum(total, axis=1, keepdims=True)
            pick = lax.broadcasted_iota(jnp.int32, (8, TILE), 0) == lax.broadcasted_iota(
                jnp.int32, (8, TILE), 1
            )
            row = jnp.sum(jnp.where(pick, lane_sum, 0.0), axis=0, keepdims=True)
            nsrc[k - 1] = row
            nrecv[k - 1, me] = row
            send_space(
                lambda peer: nsrc.at[k - 1],
                nrecv.at[k - 1, me],
                norm_s.at[k - 1],
                norm_r.at[k - 1],
            )
            sent.append((nrecv.at[k - 1], n_space - 1, norm_s.at[k - 1], norm_r.at[k - 1]))

        if k == 0:
            for copy in pos_copies:
                copy.wait_recv()
            lax.fori_loop(0, pairs, build_pair, 0)
        for copy in halo(k):
            copy.wait_recv()
        near_apply(k)

        all_but_one(rs.at[k], n_space - 1, rs_s.at[k], rs_r.at[k]).wait_recv()
        total = rs[k, 0]
        for s in range(1, n_space):
            total = total + rs[k, s]
        agb[k, me] = total
        send_space(lambda peer: agb.at[k, me], agb.at[k, me], ag_s.at[k], ag_r.at[k])
        sent.append((agb.at[k], n_space - 1, ag_s.at[k], ag_r.at[k]))
        all_but_one(agb.at[k], n_space - 1, ag_s.at[k], ag_r.at[k]).wait_recv()

        rows = [[], [], []]
        for half in range(2):
            for n in range(waves // TILE):
                at = slice(n * TILE, (n + 1) * TILE)
                chip = half * (waves // TILE) + n
                d = []
                for tangent in range(2):
                    slot = 2 * (tangent * (2 * waves // TILE) + chip)
                    d.append(jnp.concatenate([agb[k, slot], agb[k, slot + 1]], axis=0))
                rows[0].append(ev[0, :, at] * d[0] + ev[2, :, at] * d[1])
                rows[1].append(ev[1, :, at] * d[0] + ev[3, :, at] * d[1])
                rows[2].append(ev[4, :, at] * d[1])
        lhs = split_rows(
            jnp.concatenate([jnp.concatenate(r, axis=1) for r in rows], axis=0)
        )
        contract = (((1,), (1,)), ((), ()))
        for n in range(tiles // 2):
            span = slice(n * 2 * TILE, (n + 1) * 2 * TILE)
            v = lax.dot_general(
                lhs, ph_hi[span, :], contract, preferred_element_type=F32
            ) + lax.dot_general(lhs, ph_lo[span, :], contract, preferred_element_type=F32)
            v = v[0:24] + v[24:48]
            for q in range(2):
                t = 2 * n + q
                vbuf[k, t] = v[:, q * TILE : (q + 1) * TILE] + near[t]

        wr[k, wv] = vbuf[k, wv] + u[k, tiles + wv]

        def send_part(d, _):
            peer = lax.rem(wv + d, n_wave)
            remote(vbuf.at[k, peer], wr.at[k, wv], wr_s.at[k], wr_r.at[k], me, peer).start()
            return 0

        lax.fori_loop(1, n_wave, send_part, 0)
        sent.append((wr.at[k], n_wave - 1, wr_s.at[k], wr_r.at[k]))
        all_but_one(wr.at[k], n_wave - 1, wr_s.at[k], wr_r.at[k]).wait_recv()
        image = wr[k, 0]
        for w in range(1, n_wave):
            image = image + wr[k, w]

        if k < DEGREE - 1:
            own = u.at[k + 1, tiles + wv]
            u[k + 1, tiles + wv] = image
            whole = u.at[k + 1, pl.ds(tiles, tiles)]
        else:
            for j in range(2):
                all_but_one(nrecv.at[j], n_space - 1, norm_s.at[j], norm_r.at[j]).wait_recv()
            sums = []
            for j in range(2):
                total = nrecv[j, 0]
                for s in range(1, n_space):
                    total = total + nrecv[j, s]
                sums.append(total)
            ratio = jnp.max(sums[1] / (sums[0] + EPSILON), axis=1, keepdims=True)
            high = SAFETY * jnp.sqrt(jnp.broadcast_to(ratio, (8, TILE)))
            low = high / SPREAD
            nodes = DEGREE + 1
            angles = [(j + 0.5) * math.pi / nodes for j in range(nodes)]
            samples = [
                jnp.sqrt(0.5 * (high - low) * F32(math.cos(a)) + 0.5 * (high + low)) for a in angles
            ]
            coeffs = []
            for order in range(nodes):
                c = samples[0] * F32(math.cos(order * angles[0]))
                for j in range(1, nodes):
                    c = c + samples[j] * F32(math.cos(order * angles[j]))
                coeffs.append(c * F32((1.0 if order == 0 else 2.0) / nodes))
            bound_sum = high + low
            scale = 1.0 / (high - low)
            pieces = []
            for c in range(3):
                at = slice(c * 8, (c + 1) * 8)
                f = u[0, tiles + wv, at]
                u1 = u[1, tiles + wv, at]
                u2 = u[2, tiles + wv, at]
                u3 = image[at]
                t1 = (2.0 * u1 - bound_sum * f) * scale
                mt1 = (2.0 * u2 - bound_sum * u1) * scale
                mmt1 = (2.0 * u3 - bound_sum * u2) * scale
                t2 = 2.0 * (2.0 * mt1 - bound_sum * t1) * scale - f
                mt2 = 2.0 * (2.0 * mmt1 - bound_sum * mt1) * scale - u1
                t3 = 2.0 * (2.0 * mt2 - bound_sum * t2) * scale - t1
                pieces.append(coeffs[0] * f + coeffs[1] * t1 + coeffs[2] * t2 + coeffs[3] * t3)
            own = outb.at[wv]
            outb[wv] = jnp.concatenate(pieces, axis=0)
            whole = outb

        def send_tile(d, _):
            remote(own, own, wa_s.at[k], wa_r.at[k], me, lax.rem(wv + d, n_wave)).start()
            return 0

        lax.fori_loop(1, n_wave, send_tile, 0)
        sent.append((whole, n_wave - 1, wa_s.at[k], wa_r.at[k]))
        all_but_one(whole, n_wave - 1, wa_s.at[k], wa_r.at[k]).wait_recv()
        if k < DEGREE - 1:
            for copy in halo(k + 1):
                copy.start()

    out_ref[...] = outb[...]
    for ref, count, ssem, rsem in sent:
        all_but_one(ref, count, ssem, rsem).wait_send()
    for copy in pos_copies:
        copy.wait_send()
    for k in range(DEGREE):
        for copy in halo(k):
            copy.wait_send()


def body(n_space, n_wave, noise, positions, wave_index, tile_lists, tile_counts):
    tiles = positions.shape[1] // TILE
    count = positions.shape[1]
    waves = wave_index.shape[1]
    vectors = noise.shape[0]
    rows = vectors * 3
    arranged = jnp.transpose(noise, (1, 0, 2)).reshape(rows, count)
    pairs = 32 // n_wave
    vmem = pl.BlockSpec(memory_space=pltpu.VMEM)
    smem = pl.BlockSpec(memory_space=pltpu.SMEM)
    dma = pltpu.SemaphoreType.DMA

    out = pl.pallas_call(
        functools.partial(kernel, n_space, n_wave),
        out_shape=jax.ShapeDtypeStruct((tiles, rows, TILE), F32),
        in_specs=[vmem, vmem, vmem, smem, smem],
        out_specs=vmem,
        scratch_shapes=[
            pltpu.VMEM((count, 2 * waves), BF16),
            pltpu.VMEM((count, 2 * waves), BF16),
            pltpu.VMEM((3 * tiles, 8, TILE), F32),
            pltpu.VMEM((5, 8, waves), F32),
            pltpu.VMEM((3, 8, waves), F32),
            pltpu.VMEM((pairs, 3 * TILE, 3 * TILE), BF16),
            pltpu.VMEM((pairs, 3 * TILE, 3 * TILE), BF16),
            pltpu.VMEM((DEGREE, 3 * tiles, rows, TILE), F32),
            pltpu.VMEM((tiles, rows, TILE), F32),
            pltpu.VMEM((DEGREE, n_space, 4, TILE), F32),
            pltpu.VMEM((DEGREE, n_space, 4, TILE), F32),
            pltpu.VMEM((DEGREE, n_space, 4, TILE), F32),
            pltpu.VMEM((DEGREE, tiles, rows, TILE), F32),
            pltpu.VMEM((DEGREE, tiles, rows, TILE), F32),
            pltpu.VMEM((2, 1, TILE), F32),
            pltpu.VMEM((2, n_space, 1, TILE), F32),
            pltpu.VMEM((tiles, rows, TILE), F32),
            dma((DEGREE,)),
            dma((DEGREE,)),
            dma((DEGREE,)),
            dma((DEGREE,)),
            dma((DEGREE,)),
            dma((DEGREE,)),
            dma((DEGREE,)),
            dma((DEGREE,)),
            dma((DEGREE, 2)),
            dma((DEGREE, 2)),
            dma((2,)),
            dma((2,)),
            dma((2,)),
            dma((2,)),
        ],
        compiler_params=pltpu.CompilerParams(
            collective_id=0, has_side_effects=True, vmem_limit_bytes=32 * 1024 * 1024
        ),
    )(arranged, positions, wave_index, tile_lists, tile_counts)
    out = out.reshape(tiles, 3, vectors, TILE)
    return jnp.transpose(out, (2, 1, 0, 3)).reshape(vectors, 3, count)


def solution(mesh):
    n_space, n_wave = mesh.shape["space"], mesh.shape["wave"]

    def step(*args):
        return body(n_space, n_wave, *args)

    in_specs = (
        P(None, None, "space"),
        P(None, "space"),
        P(None, "wave"),
        P("space", None),
        P("space"),
    )
    out_specs = P(None, None, "space")
    return jax.shard_map(step, mesh=mesh, in_specs=in_specs, out_specs=out_specs, check_vma=False)
```

```python
import functools
import math

import jax
import jax.numpy as jnp
from jax import lax
from jax.experimental import pallas as pl
from jax.experimental.pallas import tpu as pltpu
from jax.sharding import PartitionSpec as P

MESH = pl.DeviceIdType.MESH
F32 = jnp.float32
BF16 = jnp.bfloat16

KW = 4096
DEGREE = 3
TILE = 128
SIDE_CROSS = 8.0
NEAR_SQUARE = 0.36
NEAR_AMP = 0.15
FAR_AMP = 8.0
SPLIT_SQUARE = 64.0
SCREEN = 4.0
SAFETY = 1.25
SPREAD = 100.0
EPSILON = 1e-06

SINE = (6.283185160087367, -41.34165503087954, 81.60100403735636, -76.54978142115317, 39.5366991046531)


def split_rows(x):
    high = x.astype(BF16).astype(F32)
    return jnp.concatenate([high, x - high], axis=0).astype(BF16)


def sine_of_turns(a):
    a2 = a * a
    p = F32(SINE[-1])
    for c in SINE[-2::-1]:
        p = p * a2 + F32(c)
    return p * a


def nearest(x):
    return jnp.floor(x + 0.5)


def kernel(
    n_space,
    n_wave,
    noise_hbm,
    pos_hbm,
    wave_hbm,
    lists_hbm,
    counts_hbm,
    out_ref,
    pos_ref,
    wave_ref,
    lists_ref,
    counts_ref,
    cacc,
    back,
    ph_hi,
    ph_lo,
    posw,
    ev,
    nf,
    bm_hi,
    bm_lo,
    u0,
    u1_,
    u2_,
    near,
    sbuf,
    rs,
    agb,
    vbuf,
    wr,
    nsrc,
    nrecv,
    outb,
    rs_s,
    rs_r,
    ag_s,
    ag_r,
    wr_s,
    wr_r,
    wa_s,
    wa_r,
    halo_s,
    halo_r,
    pos_s,
    pos_r,
    norm_s,
    norm_r,
    in_s,
):
    me = lax.axis_index("space")
    wv = lax.axis_index("wave")
    up = lax.rem(me + 1, n_space)
    down = lax.rem(me + n_space - 1, n_space)
    tiles = n_wave
    u = (u0, u1_, u2_)

    loads = [
        pltpu.make_async_copy(pos_hbm, pos_ref, in_s.at[0]),
        pltpu.make_async_copy(wave_hbm, wave_ref, in_s.at[1]),
    ]
    for t in range(tiles):
        loads.append(
            pltpu.make_async_copy(
                noise_hbm.at[:, pl.ds(t * TILE, TILE)], u[0].at[tiles + t], in_s.at[4 + t]
            )
        )
    loads.append(pltpu.make_async_copy(lists_hbm, lists_ref, in_s.at[2]))
    loads.append(pltpu.make_async_copy(counts_hbm, counts_ref, in_s.at[3]))
    for copy in loads:
        copy.start()

    barrier = pltpu.get_barrier_semaphore()

    def greet_space(d, _):
        pl.semaphore_signal(
            barrier, inc=1, device_id=(lax.rem(me + d, n_space), wv), device_id_type=MESH
        )
        return 0

    def greet_wave(d, _):
        pl.semaphore_signal(
            barrier, inc=1, device_id=(me, lax.rem(wv + d, n_wave)), device_id_type=MESH
        )
        return 0

    lax.fori_loop(1, n_space, greet_space, 0)
    lax.fori_loop(1, n_wave, greet_wave, 0)

    def remote(src, dst, ssem, rsem, s, w):
        return pltpu.make_async_remote_copy(
            src_ref=src,
            dst_ref=dst,
            send_sem=ssem,
            recv_sem=rsem,
            device_id=(s, w),
            device_id_type=MESH,
        )

    for copy in loads:
        copy.wait()

    for t in range(tiles):
        lanes = slice(t * TILE, (t + 1) * TILE)
        posw[tiles + t] = jnp.concatenate(
            [pos_ref[:, lanes], jnp.zeros((5, TILE), F32)], axis=0
        )

    waves = wave_ref.shape[1]
    n_all = wave_ref[...].astype(F32)
    n_rows = [jnp.broadcast_to(n_all[c : c + 1], (8, waves)) for c in range(3)]
    ka = n_rows[0] * F32(2.0 * math.pi / n_space)
    kb = n_rows[1] * F32(2.0 * math.pi / SIDE_CROSS)
    kc = n_rows[2] * F32(2.0 * math.pi / SIDE_CROSS)
    plane = ka * ka + kb * kb
    square = plane + kc * kc
    scaled = square / SPLIT_SQUARE
    weight = FAR_AMP * (1.0 + scaled) * jnp.exp(-scaled) / (KW * (square + SCREEN))
    root = jnp.sqrt(weight)
    rho = jnp.sqrt(plane)
    length = jnp.sqrt(square)
    ev[0] = -root * kb / rho
    ev[1] = root * ka / rho
    ev[2] = -root * ka * kc / (rho * length)
    ev[3] = -root * kb * kc / (rho * length)
    ev[4] = root * rho / length
    for c in range(3):
        nf[c] = n_rows[c]

    def make_phases(t, _):
        cols = jnp.transpose(posw[tiles + t])
        for j in range(TILE // 16):
            rows = pl.ds(pl.multiple_of(t * TILE + j * 16, 16), 16)
            part = cols[j * 16 : (j + 1) * 16]
            tx = part[:, 0:1] * F32(1.0 / n_space)
            ty = part[:, 1:2] * F32(1.0 / SIDE_CROSS)
            tz = part[:, 2:3] * F32(1.0 / SIDE_CROSS)
            turns = tx * nf[0, 0:1] + ty * nf[1, 0:1] + tz * nf[2, 0:1]
            r = turns - nearest(turns)
            q = r - 0.25
            q = q - nearest(q)
            cosine = sine_of_turns(0.25 - jnp.abs(r))
            sine = sine_of_turns(0.25 - jnp.abs(q))
            for at, value in ((0, cosine), (waves, sine)):
                high = value.astype(BF16)
                ph_hi[rows, at : at + waves] = high
                ph_lo[rows, at : at + waves] = (value - high.astype(F32)).astype(BF16)
        return 0

    lax.fori_loop(0, tiles // 2, make_phases, 0)

    def halo(k):
        own = u[k].at[pl.ds(tiles, tiles)]
        return (
            remote(own, u[k].at[pl.ds(0, tiles)], halo_s.at[k, 0], halo_r.at[k, 0], up, wv),
            remote(own, u[k].at[pl.ds(2 * tiles, tiles)], halo_s.at[k, 1], halo_r.at[k, 1], down, wv),
        )

    own_pos = posw.at[pl.ds(tiles, tiles)]
    pos_copies = (
        remote(own_pos, posw.at[pl.ds(0, tiles)], pos_s.at[0], pos_r.at[0], up, wv),
        remote(own_pos, posw.at[pl.ds(2 * tiles, tiles)], pos_s.at[1], pos_r.at[1], down, wv),
    )

    pl.semaphore_wait(barrier, n_space - 1 + n_wave - 1)

    for copy in pos_copies + halo(0):
        copy.start()

    lax.fori_loop(tiles // 2, tiles, make_phases, 0)

    def pair_of(i):
        j = wv * (32 // n_wave) + i
        total = jnp.int32(0)
        tile = jnp.int32(0)
        base = jnp.int32(0)
        for t in range(tiles):
            total = total + counts_ref[t]
            past = total <= j
            tile = tile + past.astype(jnp.int32)
            base = jnp.where(past, total, base)
        tile = jnp.minimum(tile, tiles - 1)
        slot = jnp.clip(j - base, 0, lists_ref.shape[1] - 1)
        return tile, jnp.clip(lists_ref[tile, slot], 0, 3 * tiles - 1)

    pairs = 32 // n_wave

    def build_pair(i, _):
        tile, source = pair_of(i)
        target_rows = posw[tiles + tile]
        source_cols = jnp.transpose(posw[source])
        offs = []
        for c, side in enumerate((float(n_space), SIDE_CROSS, SIDE_CROSS)):
            off = target_rows[c : c + 1] - source_cols[:, c : c + 1]
            offs.append(off - F32(side) * jnp.floor(off * F32(1.0 / side) + 0.5))
        square = offs[0] * offs[0] + offs[1] * offs[1] + offs[2] * offs[2]
        diagonal = lax.broadcasted_iota(jnp.int32, (TILE, TILE), 0) == lax.broadcasted_iota(
            jnp.int32, (TILE, TILE), 1
        )
        own = jnp.where(source == tiles + tile, F32(0.0), F32(1.0))
        keep = jnp.where(diagonal, own, F32(1.0))
        envelope = NEAR_AMP * jnp.exp(-square / NEAR_SQUARE) * keep
        scaled_env = envelope / NEAR_SQUARE
        for a in range(3):
            left = offs[a] * scaled_env
            for b in range(a, 3):
                block = left * offs[b]
                if a == b:
                    block = block + envelope
                high = block.astype(BF16)
                low = (block - high.astype(F32)).astype(BF16)
                for p, q in sorted({(a, b), (b, a)}):
                    at = (i, slice(p * TILE, (p + 1) * TILE), slice(q * TILE, (q + 1) * TILE))
                    bm_hi[at] = high
                    bm_lo[at] = low
        return 0

    def near_apply(k):
        near[...] = jnp.zeros_like(near)

        def one_pair(i, _):
            tile, source = pair_of(i)
            f = u[k][source]
            lhs = split_rows(jnp.concatenate([f[0:8], f[8:16], f[16:24]], axis=1))
            res = jnp.dot(lhs, bm_hi[i], preferred_element_type=F32) + jnp.dot(
                lhs, bm_lo[i], preferred_element_type=F32
            )
            res = res[0:8] + res[8:16]
            res = jnp.concatenate([res[:, c * TILE : (c + 1) * TILE] for c in range(3)], axis=0)
            for t in range(tiles):
                near[t] += jnp.where(tile == t, res, 0.0)
            return 0

        lax.fori_loop(0, pairs, one_pair, 0)

    my_y, my_x, my_c = lax.div(me, 8), lax.rem(lax.div(me, 2), 4), lax.rem(me, 2)
    far = {0: 0, 1: 1, 2: 2, 3: 1}
    steps = [(dy, dx, dc) for dy in range(4) for dx in range(4) for dc in range(2)]
    steps = sorted(steps, key=lambda d: -(10 * (far[d[0]] + far[d[1]]) + d[2]))[:-1]
    n_chips = n_space // 2
    my_chip = lax.div(me, 2)
    chip_steps = [(dy, dx) for dy in range(4) for dx in range(4)]
    chip_steps = sorted(chip_steps, key=lambda d: -(far[d[0]] + far[d[1]]))

    def chip_at(dy, dx):
        return lax.rem(my_y + dy, 4) * 4 + lax.rem(my_x + dx, 4)

    ring_order = [4, 3, 5, 2, 6, 1, 7]

    def send_space(src_of, dst, ssem, rsem):
        for dy, dx, dc in steps:
            peer = lax.rem(my_y + dy, 4) * 8 + lax.rem(my_x + dx, 4) * 2 + lax.rem(my_c + dc, 2)
            remote(src_of(peer), dst, ssem, rsem, peer, wv).start()

    def tile_at(d):
        return lax.rem(wv + d, n_wave)

    def phase_rows(ref, da, db, cols):
        parts = []
        for d in (da, db):
            rows = pl.ds(pl.multiple_of(tile_at(d) * TILE, TILE), TILE)
            parts.append(ref[rows, cols])
        return jnp.concatenate(parts, axis=0)

    def all_but_one(ref, count, ssem, rsem):
        some = ref.at[pl.ds(0, count)]
        return remote(some, some, ssem, rsem, up, wv)

    sent = []

    for k in range(DEGREE):
        step = 256
        for first, (da, db) in enumerate(((0, 1), (7, 2), (6, 3), (5, 4))):
            if k > 0:
                for d in (da, db):
                    if d > 0:
                        piece = u[k].at[tiles + tile_at(d)]
                        sem = n_wave - d
                        remote(piece, piece, wa_s.at[k - 1], wa_r.at[k - 1, sem], up, wv).wait_recv()
            x = jnp.concatenate([u[k][tiles + tile_at(da)], u[k][tiles + tile_at(db)]], axis=1)
            lhs = split_rows(x)
            for n in range(2 * waves // step):
                cols = slice(n * step, (n + 1) * step)
                c = jnp.dot(
                    lhs, phase_rows(ph_hi, da, db, cols), preferred_element_type=F32
                ) + jnp.dot(lhs, phase_rows(ph_lo, da, db, cols), preferred_element_type=F32)
                if first == 0:
                    cacc[:, cols] = c[0:24] + c[24:48]
                else:
                    cacc[:, cols] += c[0:24] + c[24:48]
        for n in range(waves // step):
            for half in range(2):
                c = cacc[:, half * waves + n * step : half * waves + (n + 1) * step]
                for q in range(step // TILE):
                    lanes = slice(q * TILE, (q + 1) * TILE)
                    at = slice(n * step + q * TILE, n * step + (q + 1) * TILE)
                    c0, c1, c2 = c[0:8, lanes], c[8:16, lanes], c[16:24, lanes]
                    d0 = ev[0, :, at] * c0 + ev[1, :, at] * c1
                    d1 = ev[2, :, at] * c0 + ev[3, :, at] * c1 + ev[4, :, at] * c2
                    chip = half * (waves // TILE) + n * (step // TILE) + q
                    for tangent, d in ((0, d0), (1, d1)):
                        sbuf[k, tangent * (2 * waves // TILE) + chip] = d
        for dy, dx in chip_steps:
            peer = chip_at(dy, dx)

            def send(peer=peer):
                remote(
                    sbuf.at[k, peer], rs.at[k, me], rs_s.at[k], rs_r.at[k], 2 * peer + 1, wv
                ).start()

            if (dy, dx) == (0, 0):
                pl.when(my_c == 0)(send)
            else:
                send()

        if k > 0:
            for copy in halo(k):
                copy.start()
        if k == 0:
            for copy in pos_copies:
                copy.wait_recv()
            lax.fori_loop(0, pairs, build_pair, 0)

        @pl.when(my_c == 1)
        def _():
            all_but_one(rs.at[k], n_space - 1, rs_s.at[k], rs_r.at[k]).wait_recv()
            rs[k, me] = sbuf[k, my_chip]
            sums = [rs[k, s] + rs[k, s + 1] for s in range(0, n_space, 2)]
            while len(sums) > 1:
                sums = [sums[s] + sums[s + 1] for s in range(0, len(sums), 2)]
            agb[k, my_chip] = sums[0]
            for dy, dx in chip_steps:
                for c in (0, 1):
                    if (dy, dx, c) != (0, 0, 1):
                        own = agb.at[k, my_chip]
                        remote(
                            own, own, ag_s.at[k], ag_r.at[k], 2 * chip_at(dy, dx) + c, wv
                        ).start()

        if k > 0:
            total = jnp.zeros((8, TILE), F32)
            for t in range(tiles):
                v = u[k][tiles + t]
                v = v * v
                total = total + (v[0:8] + v[8:16] + v[16:24])
            lane_sum = jnp.sum(total, axis=1, keepdims=True)
            pick = lax.broadcasted_iota(jnp.int32, (8, TILE), 0) == lax.broadcasted_iota(
                jnp.int32, (8, TILE), 1
            )
            row = jnp.sum(jnp.where(pick, lane_sum, 0.0), axis=0, keepdims=True)
            nsrc[k - 1] = row
            nrecv[k - 1, me] = row
            send_space(
                lambda peer: nsrc.at[k - 1],
                nrecv.at[k - 1, me],
                norm_s.at[k - 1],
                norm_r.at[k - 1],
            )
            sent.append((nrecv.at[k - 1], n_space - 1, norm_s.at[k - 1], norm_r.at[k - 1]))

        for copy in halo(k):
            copy.wait_recv()
        near_apply(k)

        @pl.when(my_c == 0)
        def _():
            all_but_one(agb.at[k], n_chips, ag_s.at[k], ag_r.at[k]).wait_recv()

        @pl.when(my_c == 1)
        def _():
            all_but_one(agb.at[k], n_chips - 1, ag_s.at[k], ag_r.at[k]).wait_recv()


        rows = [[], [], []]
        for half in range(2):
            for n in range(waves // TILE):
                at = slice(n * TILE, (n + 1) * TILE)
                chip = half * (waves // TILE) + n
                d = []
                for tangent in range(2):
                    d.append(agb[k, tangent * (2 * waves // TILE) + chip])
                rows[0].append(ev[0, :, at] * d[0] + ev[2, :, at] * d[1])
                rows[1].append(ev[1, :, at] * d[0] + ev[3, :, at] * d[1])
                rows[2].append(ev[4, :, at] * d[1])
        lhs = split_rows(
            jnp.concatenate([jnp.concatenate(r, axis=1) for r in rows], axis=0)
        )
        contract = (((1,), (1,)), ((), ()))
        every = slice(0, 2 * waves)
        back[...] = lhs

        def back_pair(i, _):
            da, db = n_wave // 2 + i, n_wave // 2 - 1 - i
            v = lax.dot_general(
                back[...], phase_rows(ph_hi, da, db, every), contract, preferred_element_type=F32
            ) + lax.dot_general(
                back[...], phase_rows(ph_lo, da, db, every), contract, preferred_element_type=F32
            )
            v = v[0:24] + v[24:48]

            def part(d, q):
                t = tile_at(d)
                vbuf[k, t] = v[:, q * TILE : (q + 1) * TILE] + near[t]
                return t

            def send(t):
                remote(vbuf.at[k, t], wr.at[k, wv], wr_s.at[k], wr_r.at[k], me, t).start()

            t = part(da, 0)
            send(t)
            t = part(db, 1)

            @pl.when(db > 0)
            def _():
                send(t)

            return 0

        lax.fori_loop(0, n_wave // 2, back_pair, 0)
        wr[k, wv] = vbuf[k, wv] + u[k][tiles + wv]
        sent.append((wr.at[k], n_wave - 1, wr_s.at[k], wr_r.at[k]))
        all_but_one(wr.at[k], n_wave - 1, wr_s.at[k], wr_r.at[k]).wait_recv()
        image = wr[k, 0]
        for w in range(1, n_wave):
            image = image + wr[k, w]

        if k < DEGREE - 1:
            own = u[k + 1].at[tiles + wv]
            u[k + 1][tiles + wv] = image
            whole = u[k + 1].at[pl.ds(tiles, tiles)]
        else:
            for j in range(2):
                all_but_one(nrecv.at[j], n_space - 1, norm_s.at[j], norm_r.at[j]).wait_recv()
            sums = []
            for j in range(2):
                total = nrecv[j, 0]
                for s in range(1, n_space):
                    total = total + nrecv[j, s]
                sums.append(total)
            ratio = jnp.max(sums[1] / (sums[0] + EPSILON), axis=1, keepdims=True)
            high = SAFETY * jnp.sqrt(jnp.broadcast_to(ratio, (8, TILE)))
            low = high / SPREAD
            nodes = DEGREE + 1
            angles = [(j + 0.5) * math.pi / nodes for j in range(nodes)]
            samples = [
                jnp.sqrt(0.5 * (high - low) * F32(math.cos(a)) + 0.5 * (high + low)) for a in angles
            ]
            coeffs = []
            for order in range(nodes):
                c = samples[0] * F32(math.cos(order * angles[0]))
                for j in range(1, nodes):
                    c = c + samples[j] * F32(math.cos(order * angles[j]))
                coeffs.append(c * F32((1.0 if order == 0 else 2.0) / nodes))
            bound_sum = high + low
            scale = 1.0 / (high - low)
            pieces = []
            for c in range(3):
                at = slice(c * 8, (c + 1) * 8)
                f = u[0][tiles + wv, at]
                u1 = u[1][tiles + wv, at]
                u2 = u[2][tiles + wv, at]
                u3 = image[at]
                t1 = (2.0 * u1 - bound_sum * f) * scale
                mt1 = (2.0 * u2 - bound_sum * u1) * scale
                mmt1 = (2.0 * u3 - bound_sum * u2) * scale
                t2 = 2.0 * (2.0 * mt1 - bound_sum * t1) * scale - f
                mt2 = 2.0 * (2.0 * mmt1 - bound_sum * mt1) * scale - u1
                t3 = 2.0 * (2.0 * mt2 - bound_sum * t2) * scale - t1
                pieces.append(coeffs[0] * f + coeffs[1] * t1 + coeffs[2] * t2 + coeffs[3] * t3)
            own = outb.at[wv]
            outb[wv] = jnp.concatenate(pieces, axis=0)
            whole = outb

        for d in ring_order:
            remote(own, own, wa_s.at[k], wa_r.at[k, d], me, tile_at(d)).start()
        sent.append((whole, n_wave - 1, wa_s.at[k], wa_r.at[k, 0]))

    out_ref[wv] = outb[wv]
    for d in (1, 7, 2, 6, 3, 5, 4):
        piece = outb.at[tile_at(d)]
        remote(piece, piece, wa_s.at[2], wa_r.at[2, n_wave - d], up, wv).wait_recv()
        out_ref[tile_at(d)] = outb[tile_at(d)]
    for k in range(DEGREE):

        @pl.when(my_c == 0)
        def _():
            all_but_one(sbuf.at[k], n_chips, rs_s.at[k], rs_r.at[k]).wait_send()

        @pl.when(my_c == 1)
        def _():
            all_but_one(sbuf.at[k], n_chips - 1, rs_s.at[k], rs_r.at[k]).wait_send()
            all_but_one(rs.at[k], n_space - 1, ag_s.at[k], ag_r.at[k]).wait_send()

    for ref, count, ssem, rsem in sent:
        all_but_one(ref, count, ssem, rsem).wait_send()
    for copy in pos_copies:
        copy.wait_send()
    for k in range(DEGREE):
        for copy in halo(k):
            copy.wait_send()


def body(n_space, n_wave, noise, positions, wave_index, tile_lists, tile_counts):
    tiles = positions.shape[1] // TILE
    count = positions.shape[1]
    waves = wave_index.shape[1]
    vectors = noise.shape[0]
    rows = vectors * 3
    arranged = jnp.transpose(noise, (1, 0, 2)).reshape(rows, count)
    pairs = 32 // n_wave
    vmem = pl.BlockSpec(memory_space=pltpu.VMEM)
    dma = pltpu.SemaphoreType.DMA

    hbm = pl.BlockSpec(memory_space=pl.ANY)
    out = pl.pallas_call(
        functools.partial(kernel, n_space, n_wave),
        out_shape=jax.ShapeDtypeStruct((tiles, rows, TILE), F32),
        in_specs=[hbm] * 5,
        out_specs=vmem,
        scratch_shapes=[
            pltpu.VMEM((3, count), F32),
            pltpu.VMEM((3, waves), jnp.int32),
            pltpu.SMEM(tile_lists.shape, jnp.int32),
            pltpu.SMEM(tile_counts.shape, jnp.int32),
            pltpu.VMEM((rows, 2 * waves), F32),
            pltpu.VMEM((2 * rows, 2 * waves), BF16),
            pltpu.VMEM((count, 2 * waves), BF16),
            pltpu.VMEM((count, 2 * waves), BF16),
            pltpu.VMEM((3 * tiles, 8, TILE), F32),
            pltpu.VMEM((5, 8, waves), F32),
            pltpu.VMEM((3, 8, waves), F32),
            pltpu.VMEM((pairs, 3 * TILE, 3 * TILE), BF16),
            pltpu.VMEM((pairs, 3 * TILE, 3 * TILE), BF16),
            pltpu.VMEM((3 * tiles, rows, TILE), F32),
            pltpu.VMEM((3 * tiles, rows, TILE), F32),
            pltpu.VMEM((3 * tiles, rows, TILE), F32),
            pltpu.VMEM((tiles, rows, TILE), F32),
            pltpu.VMEM((DEGREE, n_space // 2, 8, TILE), F32),
            pltpu.VMEM((DEGREE, n_space, 8, TILE), F32),
            pltpu.VMEM((DEGREE, n_space // 2, 8, TILE), F32),
            pltpu.VMEM((DEGREE, tiles, rows, TILE), F32),
            pltpu.VMEM((DEGREE, tiles, rows, TILE), F32),
            pltpu.VMEM((2, 1, TILE), F32),
            pltpu.VMEM((2, n_space, 1, TILE), F32),
            pltpu.VMEM((tiles, rows, TILE), F32),
            dma((DEGREE,)),
            dma((DEGREE,)),
            dma((DEGREE,)),
            dma((DEGREE,)),
            dma((DEGREE,)),
            dma((DEGREE,)),
            dma((DEGREE,)),
            dma((DEGREE, n_wave)),
            dma((DEGREE, 2)),
            dma((DEGREE, 2)),
            dma((2,)),
            dma((2,)),
            dma((2,)),
            dma((2,)),
            dma((4 + tiles,)),
        ],
        compiler_params=pltpu.CompilerParams(
            collective_id=0, has_side_effects=True, vmem_limit_bytes=60 * 1024 * 1024
        ),
    )(arranged, positions, wave_index, tile_lists, tile_counts)
    out = out.reshape(tiles, 3, vectors, TILE)
    return jnp.transpose(out, (2, 1, 0, 3)).reshape(vectors, 3, count)


def solution(mesh):
    n_space, n_wave = mesh.shape["space"], mesh.shape["wave"]

    def step(*args):
        return body(n_space, n_wave, *args)

    in_specs = (
        P(None, None, "space"),
        P(None, "space"),
        P(None, "wave"),
        P("space", None),
        P("space"),
    )
    out_specs = P(None, None, "space")
    return jax.shard_map(step, mesh=mesh, in_specs=in_specs, out_specs=out_specs, check_vma=False)
```

```python
import functools
import math

import jax
import jax.numpy as jnp
from jax import lax
from jax.experimental import pallas as pl
from jax.experimental.pallas import tpu as pltpu
from jax.sharding import PartitionSpec as P

MESH = pl.DeviceIdType.MESH
F32 = jnp.float32
BF16 = jnp.bfloat16

KW = 4096
DEGREE = 3
TILE = 128
SIDE_CROSS = 8.0
NEAR_SQUARE = 0.36
NEAR_AMP = 0.15
FAR_AMP = 8.0
SPLIT_SQUARE = 64.0
SCREEN = 4.0
SAFETY = 1.25
SPREAD = 100.0
EPSILON = 1e-06

ODD = (-6.283185160088051, 41.34165503105119, -81.60100404875506, 76.54978169659269, -39.53670129282338)
EVEN = (0.9999999534612963, -19.739171433341692, 64.93459053611144, -85.24032812693831, 56.242362994696336)


def split_rows(x):
    high = x.astype(BF16).astype(F32)
    return jnp.concatenate([high, x - high], axis=0).astype(BF16)


def polynomial(coeffs, x):
    p = F32(coeffs[-1])
    for c in coeffs[-2::-1]:
        p = p * x + F32(c)
    return p


def kernel(
    n_space,
    n_wave,
    noise_hbm,
    pos_hbm,
    wave_hbm,
    lists_hbm,
    counts_hbm,
    out_ref,
    pos_ref,
    wave_ref,
    lists_ref,
    counts_ref,
    cacc,
    back,
    ph_hi,
    ph_lo,
    pt_hi,
    pt_lo,
    posw,
    ev,
    nf,
    nt,
    pf,
    turns,
    turns_t,
    bm_hi,
    bm_lo,
    u0,
    u1_,
    u2_,
    near,
    sbuf,
    rs,
    agb,
    vbuf,
    wr,
    nsrc,
    nrecv,
    outb,
    rs_s,
    rs_r,
    ag_s,
    ag_r,
    wr_s,
    wr_r,
    wa_s,
    wa_r,
    halo_s,
    halo_r,
    pos_s,
    pos_r,
    norm_s,
    norm_r,
    in_s,
):
    me = lax.axis_index("space")
    wv = lax.axis_index("wave")
    up = lax.rem(me + 1, n_space)
    down = lax.rem(me + n_space - 1, n_space)
    tiles = n_wave
    u = (u0, u1_, u2_)

    loads = [
        pltpu.make_async_copy(pos_hbm, pos_ref, in_s.at[0]),
        pltpu.make_async_copy(wave_hbm, wave_ref, in_s.at[1]),
    ]
    for t in range(tiles):
        loads.append(
            pltpu.make_async_copy(
                noise_hbm.at[:, pl.ds(t * TILE, TILE)], u[0].at[tiles + t], in_s.at[4 + t]
            )
        )
    loads.append(pltpu.make_async_copy(lists_hbm, lists_ref, in_s.at[2]))
    loads.append(pltpu.make_async_copy(counts_hbm, counts_ref, in_s.at[3]))
    for copy in loads:
        copy.start()

    barrier = pltpu.get_barrier_semaphore()

    def greet_space(d, _):
        pl.semaphore_signal(
            barrier, inc=1, device_id=(lax.rem(me + d, n_space), wv), device_id_type=MESH
        )
        return 0

    def greet_wave(d, _):
        pl.semaphore_signal(
            barrier, inc=1, device_id=(me, lax.rem(wv + d, n_wave)), device_id_type=MESH
        )
        return 0

    lax.fori_loop(1, n_space, greet_space, 0)
    lax.fori_loop(1, n_wave, greet_wave, 0)

    def remote(src, dst, ssem, rsem, s, w):
        return pltpu.make_async_remote_copy(
            src_ref=src,
            dst_ref=dst,
            send_sem=ssem,
            recv_sem=rsem,
            device_id=(s, w),
            device_id_type=MESH,
        )

    for copy in loads[:2]:
        copy.wait()

    for t in range(tiles):
        lanes = slice(t * TILE, (t + 1) * TILE)
        posw[tiles + t] = jnp.concatenate(
            [pos_ref[:, lanes], jnp.zeros((5, TILE), F32)], axis=0
        )

    waves = wave_ref.shape[1]
    n_all = wave_ref[...].astype(F32)
    n_rows = [jnp.broadcast_to(n_all[c : c + 1], (8, waves)) for c in range(3)]
    ka = n_rows[0] * F32(2.0 * math.pi / n_space)
    kb = n_rows[1] * F32(2.0 * math.pi / SIDE_CROSS)
    kc = n_rows[2] * F32(2.0 * math.pi / SIDE_CROSS)
    plane = ka * ka + kb * kb
    square = plane + kc * kc
    scaled = square / SPLIT_SQUARE
    weight = FAR_AMP * (1.0 + scaled) * jnp.exp(-scaled) / (KW * (square + SCREEN))
    root = jnp.sqrt(weight)
    rho = jnp.sqrt(plane)
    length = jnp.sqrt(square)
    ev[0] = -root * kb / rho
    ev[1] = root * ka / rho
    ev[2] = -root * ka * kc / (rho * length)
    ev[3] = -root * kb * kc / (rho * length)
    ev[4] = root * rho / length
    padded = jnp.concatenate([n_all, jnp.zeros((5, waves), F32)], axis=0)
    padded = jnp.concatenate([padded] * 3, axis=0)
    nf[...] = padded.astype(BF16)
    for n in range(waves // TILE):
        at = slice(n * TILE, (n + 1) * TILE)
        nt[at, :] = jnp.transpose(padded[:, at]).astype(BF16)
    sides = jnp.where(
        lax.broadcasted_iota(jnp.int32, (8, TILE), 0) == 0, F32(1.0 / n_space), F32(1.0 / SIDE_CROSS)
    )

    def trig(angle):
        r = angle - jnp.floor(angle + 0.5)
        b = jnp.abs(r) - 0.25
        b2 = b * b
        cosine = polynomial(ODD, b2) * b
        sine = polynomial(EVEN, b2)
        sine = jnp.where(r < 0.0, -sine, sine)
        halves = []
        for value in (cosine, sine):
            high = value.astype(BF16)
            halves.append((high, (value - high.astype(F32)).astype(BF16)))
        return halves

    def make_phases(t):
        box = posw[tiles + t] * sides
        first = box.astype(BF16).astype(F32)
        second = (box - first).astype(BF16).astype(F32)
        pieces = jnp.concatenate([first, second, box - first - second], axis=0)
        pf[:, pl.ds(pl.multiple_of(t * TILE, TILE), TILE)] = pieces.astype(BF16)
        turns[...] = jnp.dot(
            jnp.transpose(pieces).astype(BF16), nf[...], preferred_element_type=F32
        )
        for j in range(TILE // 16):
            rows = pl.ds(pl.multiple_of(t * TILE + j * 16, 16), 16)
            for at, (high, low) in zip((0, waves), trig(turns[j * 16 : (j + 1) * 16])):
                ph_hi[rows, at : at + waves] = high
                ph_lo[rows, at : at + waves] = low

    def make_transposed(n, _):
        block = nt[pl.ds(pl.multiple_of(n * TILE, TILE), TILE), :]
        turns_t[...] = jnp.dot(block, pf[...], preferred_element_type=F32)
        for j in range(TILE // 16):
            for half in range(2):
                lanes = slice(half * waves, (half + 1) * waves)
                parts = trig(turns_t[j * 16 : (j + 1) * 16, lanes])
                for at, (high, low) in zip((0, waves), parts):
                    rows = pl.ds(pl.multiple_of(at + n * TILE + j * 16, 16), 16)
                    pt_hi[rows, lanes] = high
                    pt_lo[rows, lanes] = low
        return 0

    step = 256

    def fold(t):
        lhs = split_rows(u[0][tiles + t])
        rows = pl.ds(pl.multiple_of(t * TILE, TILE), TILE)
        for n in range(2 * waves // step):
            cols = slice(n * step, (n + 1) * step)
            c = jnp.dot(lhs, ph_hi[rows, cols], preferred_element_type=F32) + jnp.dot(
                lhs, ph_lo[rows, cols], preferred_element_type=F32
            )
            cacc[:, cols] += c[0:24] + c[24:48]

    def fold_and_make(t, _):
        fold(t - 1)
        make_phases(t)
        return 0

    cacc[...] = jnp.zeros_like(cacc)
    make_phases(0)
    for copy in loads[2:]:
        copy.wait()
    lax.fori_loop(1, tiles, fold_and_make, 0)
    fold(tiles - 1)

    def halo(k):
        own = u[k].at[pl.ds(tiles, tiles)]
        return (
            remote(own, u[k].at[pl.ds(0, tiles)], halo_s.at[k, 0], halo_r.at[k, 0], up, wv),
            remote(own, u[k].at[pl.ds(2 * tiles, tiles)], halo_s.at[k, 1], halo_r.at[k, 1], down, wv),
        )

    own_pos = posw.at[pl.ds(tiles, tiles)]
    pos_copies = (
        remote(own_pos, posw.at[pl.ds(0, tiles)], pos_s.at[0], pos_r.at[0], up, wv),
        remote(own_pos, posw.at[pl.ds(2 * tiles, tiles)], pos_s.at[1], pos_r.at[1], down, wv),
    )

    def pair_of(i):
        j = wv * (32 // n_wave) + i
        total = jnp.int32(0)
        tile = jnp.int32(0)
        base = jnp.int32(0)
        for t in range(tiles):
            total = total + counts_ref[t]
            past = total <= j
            tile = tile + past.astype(jnp.int32)
            base = jnp.where(past, total, base)
        tile = jnp.minimum(tile, tiles - 1)
        slot = jnp.clip(j - base, 0, lists_ref.shape[1] - 1)
        return tile, jnp.clip(lists_ref[tile, slot], 0, 3 * tiles - 1)

    pairs = 32 // n_wave

    def build_pair(i, _):
        tile, source = pair_of(i)
        target_rows = posw[tiles + tile]
        source_cols = jnp.transpose(posw[source])
        offs = []
        for c, side in enumerate((float(n_space), SIDE_CROSS, SIDE_CROSS)):
            off = target_rows[c : c + 1] - source_cols[:, c : c + 1]
            offs.append(off - F32(side) * jnp.floor(off * F32(1.0 / side) + 0.5))
        square = offs[0] * offs[0] + offs[1] * offs[1] + offs[2] * offs[2]
        diagonal = lax.broadcasted_iota(jnp.int32, (TILE, TILE), 0) == lax.broadcasted_iota(
            jnp.int32, (TILE, TILE), 1
        )
        own = jnp.where(source == tiles + tile, F32(0.0), F32(1.0))
        keep = jnp.where(diagonal, own, F32(1.0))
        envelope = NEAR_AMP * jnp.exp(-square / NEAR_SQUARE) * keep
        scaled_env = envelope / NEAR_SQUARE
        for a in range(3):
            left = offs[a] * scaled_env
            for b in range(a, 3):
                block = left * offs[b]
                if a == b:
                    block = block + envelope
                high = block.astype(BF16)
                low = (block - high.astype(F32)).astype(BF16)
                for p, q in sorted({(a, b), (b, a)}):
                    at = (i, slice(p * TILE, (p + 1) * TILE), slice(q * TILE, (q + 1) * TILE))
                    bm_hi[at] = high
                    bm_lo[at] = low
        return 0

    def near_apply(k):
        near[...] = jnp.zeros_like(near)

        def one_pair(i, _):
            tile, source = pair_of(i)
            f = u[k][source]
            lhs = split_rows(jnp.concatenate([f[0:8], f[8:16], f[16:24]], axis=1))
            res = jnp.dot(lhs, bm_hi[i], preferred_element_type=F32) + jnp.dot(
                lhs, bm_lo[i], preferred_element_type=F32
            )
            res = res[0:8] + res[8:16]
            res = jnp.concatenate([res[:, c * TILE : (c + 1) * TILE] for c in range(3)], axis=0)
            for t in range(tiles):
                near[t] += jnp.where(tile == t, res, 0.0)
            return 0

        lax.fori_loop(0, pairs, one_pair, 0)

    my_y, my_x, my_c = lax.div(me, 8), lax.rem(lax.div(me, 2), 4), lax.rem(me, 2)
    far = {0: 0, 1: 1, 2: 2, 3: 1}
    steps = [(dy, dx, dc) for dy in range(4) for dx in range(4) for dc in range(2)]
    steps = sorted(steps, key=lambda d: -(10 * (far[d[0]] + far[d[1]]) + d[2]))[:-1]
    n_chips = n_space // 2
    my_chip = lax.div(me, 2)
    chip_steps = [(dy, dx) for dy in range(4) for dx in range(4)]
    chip_steps = sorted(chip_steps, key=lambda d: -(far[d[0]] + far[d[1]]))

    def chip_at(dy, dx):
        return lax.rem(my_y + dy, 4) * 4 + lax.rem(my_x + dx, 4)

    ring_order = [4, 3, 5, 2, 6, 1, 7]

    def send_space(src_of, dst, ssem, rsem):
        for dy, dx, dc in steps:
            peer = lax.rem(my_y + dy, 4) * 8 + lax.rem(my_x + dx, 4) * 2 + lax.rem(my_c + dc, 2)
            remote(src_of(peer), dst, ssem, rsem, peer, wv).start()

    def tile_at(d):
        return lax.rem(wv + d, n_wave)

    def phase_cols(ref, da, db):
        parts = []
        for d in (da, db):
            cols = pl.ds(pl.multiple_of(tile_at(d) * TILE, TILE), TILE)
            parts.append(ref[:, cols])
        return jnp.concatenate(parts, axis=1)

    def phase_rows(ref, da, db, cols):
        parts = []
        for d in (da, db):
            rows = pl.ds(pl.multiple_of(tile_at(d) * TILE, TILE), TILE)
            parts.append(ref[rows, cols])
        return jnp.concatenate(parts, axis=0)

    def all_but_one(ref, count, ssem, rsem):
        some = ref.at[pl.ds(0, count)]
        return remote(some, some, ssem, rsem, up, wv)

    sent = []

    for k in range(DEGREE):
        for first, (da, db) in enumerate(((0, 1), (7, 2), (6, 3), (5, 4)) if k > 0 else ()):
            for d in (da, db):
                if d > 0:
                    piece = u[k].at[tiles + tile_at(d)]
                    sem = n_wave - d
                    remote(piece, piece, wa_s.at[k - 1], wa_r.at[k - 1, sem], up, wv).wait_recv()
            x = jnp.concatenate([u[k][tiles + tile_at(da)], u[k][tiles + tile_at(db)]], axis=1)
            lhs = split_rows(x)
            for n in range(2 * waves // step):
                cols = slice(n * step, (n + 1) * step)
                c = jnp.dot(
                    lhs, phase_rows(ph_hi, da, db, cols), preferred_element_type=F32
                ) + jnp.dot(lhs, phase_rows(ph_lo, da, db, cols), preferred_element_type=F32)
                if first == 0:
                    cacc[:, cols] = c[0:24] + c[24:48]
                else:
                    cacc[:, cols] += c[0:24] + c[24:48]
        for n in range(waves // step):
            for half in range(2):
                c = cacc[:, half * waves + n * step : half * waves + (n + 1) * step]
                for q in range(step // TILE):
                    lanes = slice(q * TILE, (q + 1) * TILE)
                    at = slice(n * step + q * TILE, n * step + (q + 1) * TILE)
                    c0, c1, c2 = c[0:8, lanes], c[8:16, lanes], c[16:24, lanes]
                    d0 = ev[0, :, at] * c0 + ev[1, :, at] * c1
                    d1 = ev[2, :, at] * c0 + ev[3, :, at] * c1 + ev[4, :, at] * c2
                    chip = half * (waves // TILE) + n * (step // TILE) + q
                    for tangent, d in ((0, d0), (1, d1)):
                        sbuf[k, tangent * (2 * waves // TILE) + chip] = d
        if k == 0:
            pl.semaphore_wait(barrier, n_space - 1 + n_wave - 1)
        for dy, dx in chip_steps:
            peer = chip_at(dy, dx)

            def send(peer=peer):
                remote(
                    sbuf.at[k, peer], rs.at[k, me], rs_s.at[k], rs_r.at[k], 2 * peer + 1, wv
                ).start()

            if (dy, dx) == (0, 0):
                pl.when(my_c == 0)(send)
            else:
                send()

        for copy in (pos_copies if k == 0 else ()) + halo(k):
            copy.start()
        if k == 0:
            lax.fori_loop(0, waves // TILE, make_transposed, 0)

        @pl.when(my_c == 1)
        def _():
            all_but_one(rs.at[k], n_space - 1, rs_s.at[k], rs_r.at[k]).wait_recv()
            rs[k, me] = sbuf[k, my_chip]
            sums = [rs[k, s] + rs[k, s + 1] for s in range(0, n_space, 2)]
            while len(sums) > 1:
                sums = [sums[s] + sums[s + 1] for s in range(0, len(sums), 2)]
            agb[k, my_chip] = sums[0]
            for dy, dx in chip_steps:
                for c in (0, 1):
                    if (dy, dx, c) != (0, 0, 1):
                        own = agb.at[k, my_chip]
                        remote(
                            own, own, ag_s.at[k], ag_r.at[k], 2 * chip_at(dy, dx) + c, wv
                        ).start()

        if k > 0:
            total = jnp.zeros((8, TILE), F32)
            for t in range(tiles):
                v = u[k][tiles + t]
                v = v * v
                total = total + (v[0:8] + v[8:16] + v[16:24])
            lane_sum = jnp.sum(total, axis=1, keepdims=True)
            pick = lax.broadcasted_iota(jnp.int32, (8, TILE), 0) == lax.broadcasted_iota(
                jnp.int32, (8, TILE), 1
            )
            row = jnp.sum(jnp.where(pick, lane_sum, 0.0), axis=0, keepdims=True)
            nsrc[k - 1] = row
            nrecv[k - 1, me] = row
            send_space(
                lambda peer: nsrc.at[k - 1],
                nrecv.at[k - 1, me],
                norm_s.at[k - 1],
                norm_r.at[k - 1],
            )
            sent.append((nrecv.at[k - 1], n_space - 1, norm_s.at[k - 1], norm_r.at[k - 1]))

        if k == 0:
            for copy in pos_copies:
                copy.wait_recv()
            lax.fori_loop(0, pairs, build_pair, 0)
        for copy in halo(k):
            copy.wait_recv()
        near_apply(k)

        @pl.when(my_c == 0)
        def _():
            all_but_one(agb.at[k], n_chips, ag_s.at[k], ag_r.at[k]).wait_recv()

        @pl.when(my_c == 1)
        def _():
            all_but_one(agb.at[k], n_chips - 1, ag_s.at[k], ag_r.at[k]).wait_recv()


        rows = [[], [], []]
        for half in range(2):
            for n in range(waves // TILE):
                at = slice(n * TILE, (n + 1) * TILE)
                chip = half * (waves // TILE) + n
                d = []
                for tangent in range(2):
                    d.append(agb[k, tangent * (2 * waves // TILE) + chip])
                rows[0].append(ev[0, :, at] * d[0] + ev[2, :, at] * d[1])
                rows[1].append(ev[1, :, at] * d[0] + ev[3, :, at] * d[1])
                rows[2].append(ev[4, :, at] * d[1])
        lhs = split_rows(
            jnp.concatenate([jnp.concatenate(r, axis=1) for r in rows], axis=0)
        )
        back[...] = lhs

        def back_pair(i, _):
            da, db = n_wave // 2 + i, n_wave // 2 - 1 - i
            v = jnp.dot(back[...], phase_cols(pt_hi, da, db), preferred_element_type=F32) + jnp.dot(
                back[...], phase_cols(pt_lo, da, db), preferred_element_type=F32
            )
            v = v[0:24] + v[24:48]

            def part(d, q):
                t = tile_at(d)
                vbuf[k, t] = v[:, q * TILE : (q + 1) * TILE] + near[t]
                return t

            def send(t):
                remote(vbuf.at[k, t], wr.at[k, wv], wr_s.at[k], wr_r.at[k], me, t).start()

            t = part(da, 0)
            send(t)
            t = part(db, 1)

            @pl.when(db > 0)
            def _():
                send(t)

            return 0

        lax.fori_loop(0, n_wave // 2, back_pair, 0)
        wr[k, wv] = vbuf[k, wv] + u[k][tiles + wv]
        sent.append((wr.at[k], n_wave - 1, wr_s.at[k], wr_r.at[k]))
        all_but_one(wr.at[k], n_wave - 1, wr_s.at[k], wr_r.at[k]).wait_recv()
        image = wr[k, 0]
        for w in range(1, n_wave):
            image = image + wr[k, w]

        if k < DEGREE - 1:
            own = u[k + 1].at[tiles + wv]
            u[k + 1][tiles + wv] = image
            whole = u[k + 1].at[pl.ds(tiles, tiles)]
        else:
            for j in range(2):
                all_but_one(nrecv.at[j], n_space - 1, norm_s.at[j], norm_r.at[j]).wait_recv()
            sums = []
            for j in range(2):
                total = nrecv[j, 0]
                for s in range(1, n_space):
                    total = total + nrecv[j, s]
                sums.append(total)
            ratio = jnp.max(sums[1] / (sums[0] + EPSILON), axis=1, keepdims=True)
            high = SAFETY * jnp.sqrt(jnp.broadcast_to(ratio, (8, TILE)))
            low = high / SPREAD
            nodes = DEGREE + 1
            angles = [(j + 0.5) * math.pi / nodes for j in range(nodes)]
            samples = [
                jnp.sqrt(0.5 * (high - low) * F32(math.cos(a)) + 0.5 * (high + low)) for a in angles
            ]
            coeffs = []
            for order in range(nodes):
                c = samples[0] * F32(math.cos(order * angles[0]))
                for j in range(1, nodes):
                    c = c + samples[j] * F32(math.cos(order * angles[j]))
                coeffs.append(c * F32((1.0 if order == 0 else 2.0) / nodes))
            bound_sum = high + low
            scale = 1.0 / (high - low)
            pieces = []
            for c in range(3):
                at = slice(c * 8, (c + 1) * 8)
                f = u[0][tiles + wv, at]
                u1 = u[1][tiles + wv, at]
                u2 = u[2][tiles + wv, at]
                u3 = image[at]
                t1 = (2.0 * u1 - bound_sum * f) * scale
                mt1 = (2.0 * u2 - bound_sum * u1) * scale
                mmt1 = (2.0 * u3 - bound_sum * u2) * scale
                t2 = 2.0 * (2.0 * mt1 - bound_sum * t1) * scale - f
                mt2 = 2.0 * (2.0 * mmt1 - bound_sum * mt1) * scale - u1
                t3 = 2.0 * (2.0 * mt2 - bound_sum * t2) * scale - t1
                pieces.append(coeffs[0] * f + coeffs[1] * t1 + coeffs[2] * t2 + coeffs[3] * t3)
            own = outb.at[wv]
            outb[wv] = jnp.concatenate(pieces, axis=0)
            whole = outb

        for d in ring_order:
            remote(own, own, wa_s.at[k], wa_r.at[k, d], me, tile_at(d)).start()
        sent.append((whole, n_wave - 1, wa_s.at[k], wa_r.at[k, 0]))

    out_ref[wv] = outb[wv]
    for d in (1, 7, 2, 6, 3, 5, 4):
        piece = outb.at[tile_at(d)]
        remote(piece, piece, wa_s.at[2], wa_r.at[2, n_wave - d], up, wv).wait_recv()
        out_ref[tile_at(d)] = outb[tile_at(d)]
    for k in range(DEGREE):

        @pl.when(my_c == 0)
        def _():
            all_but_one(sbuf.at[k], n_chips, rs_s.at[k], rs_r.at[k]).wait_send()

        @pl.when(my_c == 1)
        def _():
            all_but_one(sbuf.at[k], n_chips - 1, rs_s.at[k], rs_r.at[k]).wait_send()
            all_but_one(rs.at[k], n_space - 1, ag_s.at[k], ag_r.at[k]).wait_send()

    for ref, count, ssem, rsem in sent:
        all_but_one(ref, count, ssem, rsem).wait_send()
    for copy in pos_copies:
        copy.wait_send()
    for k in range(DEGREE):
        for copy in halo(k):
            copy.wait_send()


def body(n_space, n_wave, noise, positions, wave_index, tile_lists, tile_counts):
    tiles = positions.shape[1] // TILE
    count = positions.shape[1]
    waves = wave_index.shape[1]
    vectors = noise.shape[0]
    rows = vectors * 3
    arranged = jnp.transpose(noise, (1, 0, 2)).reshape(rows, count)
    pairs = 32 // n_wave
    vmem = pl.BlockSpec(memory_space=pltpu.VMEM)
    dma = pltpu.SemaphoreType.DMA

    hbm = pl.BlockSpec(memory_space=pl.ANY)
    out = pl.pallas_call(
        functools.partial(kernel, n_space, n_wave),
        out_shape=jax.ShapeDtypeStruct((tiles, rows, TILE), F32),
        in_specs=[hbm] * 5,
        out_specs=vmem,
        scratch_shapes=[
            pltpu.VMEM((3, count), F32),
            pltpu.VMEM((3, waves), jnp.int32),
            pltpu.SMEM(tile_lists.shape, jnp.int32),
            pltpu.SMEM(tile_counts.shape, jnp.int32),
            pltpu.VMEM((rows, 2 * waves), F32),
            pltpu.VMEM((2 * rows, 2 * waves), BF16),
            pltpu.VMEM((count, 2 * waves), BF16),
            pltpu.VMEM((count, 2 * waves), BF16),
            pltpu.VMEM((2 * waves, count), BF16),
            pltpu.VMEM((2 * waves, count), BF16),
            pltpu.VMEM((3 * tiles, 8, TILE), F32),
            pltpu.VMEM((5, 8, waves), F32),
            pltpu.VMEM((24, waves), BF16),
            pltpu.VMEM((waves, 24), BF16),
            pltpu.VMEM((24, count), BF16),
            pltpu.VMEM((TILE, waves), F32),
            pltpu.VMEM((TILE, count), F32),
            pltpu.VMEM((pairs, 3 * TILE, 3 * TILE), BF16),
            pltpu.VMEM((pairs, 3 * TILE, 3 * TILE), BF16),
            pltpu.VMEM((3 * tiles, rows, TILE), F32),
            pltpu.VMEM((3 * tiles, rows, TILE), F32),
            pltpu.VMEM((3 * tiles, rows, TILE), F32),
            pltpu.VMEM((tiles, rows, TILE), F32),
            pltpu.VMEM((DEGREE, n_space // 2, 8, TILE), F32),
            pltpu.VMEM((DEGREE, n_space, 8, TILE), F32),
            pltpu.VMEM((DEGREE, n_space // 2, 8, TILE), F32),
            pltpu.VMEM((DEGREE, tiles, rows, TILE), F32),
            pltpu.VMEM((DEGREE, tiles, rows, TILE), F32),
            pltpu.VMEM((2, 1, TILE), F32),
            pltpu.VMEM((2, n_space, 1, TILE), F32),
            pltpu.VMEM((tiles, rows, TILE), F32),
            dma((DEGREE,)),
            dma((DEGREE,)),
            dma((DEGREE,)),
            dma((DEGREE,)),
            dma((DEGREE,)),
            dma((DEGREE,)),
            dma((DEGREE,)),
            dma((DEGREE, n_wave)),
            dma((DEGREE, 2)),
            dma((DEGREE, 2)),
            dma((2,)),
            dma((2,)),
            dma((2,)),
            dma((2,)),
            dma((4 + tiles,)),
        ],
        compiler_params=pltpu.CompilerParams(
            collective_id=0, has_side_effects=True, vmem_limit_bytes=60 * 1024 * 1024
        ),
    )(arranged, positions, wave_index, tile_lists, tile_counts)
    out = out.reshape(tiles, 3, vectors, TILE)
    return jnp.transpose(out, (2, 1, 0, 3)).reshape(vectors, 3, count)


def solution(mesh):
    n_space, n_wave = mesh.shape["space"], mesh.shape["wave"]

    def step(*args):
        return body(n_space, n_wave, *args)

    in_specs = (
        P(None, None, "space"),
        P(None, "space"),
        P(None, "wave"),
        P("space", None),
        P("space"),
    )
    out_specs = P(None, None, "space")
    return jax.shard_map(step, mesh=mesh, in_specs=in_specs, out_specs=out_specs, check_vma=False)
```

```python
import functools
import math

import jax
import jax.numpy as jnp
from jax import lax
from jax.experimental import pallas as pl
from jax.experimental.pallas import tpu as pltpu
from jax.sharding import PartitionSpec as P

MESH = pl.DeviceIdType.MESH
F32 = jnp.float32
BF16 = jnp.bfloat16

KW = 4096
DEGREE = 3
TILE = 128
SIDE_CROSS = 8.0
NEAR_SQUARE = 0.36
NEAR_AMP = 0.15
FAR_AMP = 8.0
SPLIT_SQUARE = 64.0
SCREEN = 4.0
SAFETY = 1.25
SPREAD = 100.0
EPSILON = 1e-06

ODD = (4.442882834148948, -7.308241154482914, 3.6062889571583123, -0.8457635896353835, 0.10920574060672703)
EVEN = (1.4142134965574307, -6.978850987759868, 5.7394611627073875, -1.8835629390376682, 0.31069809581455876)


def split_rows(x):
    high = x.astype(BF16).astype(F32)
    return jnp.concatenate([high, x - high], axis=0).astype(BF16)


def nearest(x):
    return lax.round(x, lax.RoundingMethod.TO_NEAREST_EVEN)


def polynomial(coeffs, x):
    p = F32(coeffs[-1])
    for c in coeffs[-2::-1]:
        p = p * x + F32(c)
    return p


def kernel(
    n_space,
    n_wave,
    noise_hbm,
    pos_hbm,
    wave_hbm,
    lists_hbm,
    counts_hbm,
    out_ref,
    pos_ref,
    wave_ref,
    lists_ref,
    counts_ref,
    cacc,
    back,
    ph_hi,
    ph_lo,
    pt_hi,
    pt_lo,
    posw,
    ev,
    nf,
    nt,
    pf,
    turns,
    turns_t,
    bm_hi,
    bm_lo,
    u0,
    u1_,
    u2_,
    near,
    sbuf,
    rs,
    agb,
    vbuf,
    wr,
    nsrc,
    nrecv,
    outb,
    rs_s,
    rs_r,
    ag_s,
    ag_r,
    wr_s,
    wr_r,
    wa_s,
    wa_r,
    halo_s,
    halo_r,
    pos_s,
    pos_r,
    norm_s,
    norm_r,
    in_s,
):
    me = lax.axis_index("space")
    wv = lax.axis_index("wave")
    up = lax.rem(me + 1, n_space)
    down = lax.rem(me + n_space - 1, n_space)
    tiles = n_wave
    u = (u0, u1_, u2_)

    loads = [
        pltpu.make_async_copy(pos_hbm, pos_ref, in_s.at[0]),
        pltpu.make_async_copy(wave_hbm, wave_ref, in_s.at[1]),
    ]
    for t in range(tiles):
        loads.append(
            pltpu.make_async_copy(
                noise_hbm.at[:, pl.ds(t * TILE, TILE)], u[0].at[tiles + t], in_s.at[4 + t]
            )
        )
    loads.append(pltpu.make_async_copy(lists_hbm, lists_ref, in_s.at[2]))
    loads.append(pltpu.make_async_copy(counts_hbm, counts_ref, in_s.at[3]))
    for copy in loads:
        copy.start()

    barrier = pltpu.get_barrier_semaphore()

    def greet_space(d, _):
        pl.semaphore_signal(
            barrier, inc=1, device_id=(lax.rem(me + d, n_space), wv), device_id_type=MESH
        )
        return 0

    def greet_wave(d, _):
        pl.semaphore_signal(
            barrier, inc=1, device_id=(me, lax.rem(wv + d, n_wave)), device_id_type=MESH
        )
        return 0

    lax.fori_loop(1, n_space, greet_space, 0)
    lax.fori_loop(1, n_wave, greet_wave, 0)

    def remote(src, dst, ssem, rsem, s, w):
        return pltpu.make_async_remote_copy(
            src_ref=src,
            dst_ref=dst,
            send_sem=ssem,
            recv_sem=rsem,
            device_id=(s, w),
            device_id_type=MESH,
        )

    for copy in loads[:2]:
        copy.wait()

    for t in range(tiles):
        lanes = slice(t * TILE, (t + 1) * TILE)
        posw[tiles + t] = jnp.concatenate(
            [pos_ref[:, lanes], jnp.zeros((5, TILE), F32)], axis=0
        )

    waves = wave_ref.shape[1]
    n_all = wave_ref[...].astype(F32)
    n_rows = [jnp.broadcast_to(n_all[c : c + 1], (8, waves)) for c in range(3)]
    ka = n_rows[0] * F32(2.0 * math.pi / n_space)
    kb = n_rows[1] * F32(2.0 * math.pi / SIDE_CROSS)
    kc = n_rows[2] * F32(2.0 * math.pi / SIDE_CROSS)
    plane = ka * ka + kb * kb
    square = plane + kc * kc
    scaled = square / SPLIT_SQUARE
    weight = FAR_AMP * (1.0 + scaled) * jnp.exp(-scaled) / (KW * (square + SCREEN))
    root = jnp.sqrt(weight)
    rho = jnp.sqrt(plane)
    length = jnp.sqrt(square)
    ev[0] = -root * kb / rho
    ev[1] = root * ka / rho
    ev[2] = -root * ka * kc / (rho * length)
    ev[3] = -root * kb * kc / (rho * length)
    ev[4] = root * rho / length
    padded = jnp.concatenate([n_all, jnp.zeros((5, waves), F32)], axis=0)
    padded = jnp.concatenate([padded] * 3, axis=0)
    nf[...] = padded.astype(BF16)
    for n in range(waves // TILE):
        at = slice(n * TILE, (n + 1) * TILE)
        nt[at, :] = jnp.transpose(padded[:, at]).astype(BF16)
    sides = jnp.where(
        lax.broadcasted_iota(jnp.int32, (8, TILE), 0) == 0, F32(1.0 / n_space), F32(1.0 / SIDE_CROSS)
    )

    def trig(angle):
        r = angle - nearest(angle)
        r2 = r * r
        half_sine = polynomial(ODD, r2) * r
        cosine = 1.0 - half_sine * half_sine
        sine = half_sine * polynomial(EVEN, r2)
        halves = []
        for value in (cosine, sine):
            high = value.astype(BF16)
            halves.append((high, (value - high.astype(F32)).astype(BF16)))
        return halves

    def tile_at(d):
        return lax.rem(wv + d, n_wave)

    def distance(j):
        if isinstance(j, int):
            return (j + 1) // 2 if j % 2 == 1 else (n_wave - j // 2) % n_wave
        half = lax.div(j + 1, 2)
        return jnp.where(lax.rem(j, 2) == 1, half, lax.rem(n_wave - half, n_wave))

    def make_phases(t):
        box = posw[tiles + tile_at(distance(t))] * sides
        first = box.astype(BF16).astype(F32)
        second = (box - first).astype(BF16).astype(F32)
        pieces = jnp.concatenate([first, second, box - first - second], axis=0)
        pf[:, pl.ds(pl.multiple_of(t * TILE, TILE), TILE)] = pieces.astype(BF16)
        turns[...] = jnp.dot(
            jnp.transpose(pieces).astype(BF16), nf[...], preferred_element_type=F32
        )
        for j in range(TILE // 16):
            rows = pl.ds(pl.multiple_of(t * TILE + j * 16, 16), 16)
            for at, (high, low) in zip((0, waves), trig(turns[j * 16 : (j + 1) * 16])):
                ph_hi[rows, at : at + waves] = high
                ph_lo[rows, at : at + waves] = low

    def make_transposed(n, _):
        block = nt[pl.ds(pl.multiple_of(n * TILE, TILE), TILE), :]
        turns_t[...] = jnp.dot(block, pf[...], preferred_element_type=F32)
        for j in range(TILE // 16):
            for pair in range(tiles // 2):
                lanes = slice(pair * 2 * TILE, (pair + 1) * 2 * TILE)
                parts = trig(turns_t[j * 16 : (j + 1) * 16, lanes])
                for at, (high, low) in zip((0, waves), parts):
                    rows = pl.ds(pl.multiple_of(at + n * TILE + j * 16, 16), 16)
                    pt_hi[pair, rows, :] = high
                    pt_lo[pair, rows, :] = low
        return 0

    step = 256

    def fold(t):
        lhs = split_rows(u[0][tiles + tile_at(distance(t))])
        rows = pl.ds(pl.multiple_of(t * TILE, TILE), TILE)
        for n in range(2 * waves // step):
            cols = slice(n * step, (n + 1) * step)
            c = jnp.dot(lhs, ph_hi[rows, cols], preferred_element_type=F32) + jnp.dot(
                lhs, ph_lo[rows, cols], preferred_element_type=F32
            )
            cacc[:, cols] += c[0:24] + c[24:48]

    def fold_and_make(t, _):
        fold(t - 1)
        make_phases(t)
        return 0

    cacc[...] = jnp.zeros_like(cacc)
    make_phases(0)
    for copy in loads[2:]:
        copy.wait()
    lax.fori_loop(1, tiles, fold_and_make, 0)
    fold(tiles - 1)

    def halo(k):
        own = u[k].at[pl.ds(tiles, tiles)]
        return (
            remote(own, u[k].at[pl.ds(0, tiles)], halo_s.at[k, 0], halo_r.at[k, 0], up, wv),
            remote(own, u[k].at[pl.ds(2 * tiles, tiles)], halo_s.at[k, 1], halo_r.at[k, 1], down, wv),
        )

    own_pos = posw.at[pl.ds(tiles, tiles)]
    pos_copies = (
        remote(own_pos, posw.at[pl.ds(0, tiles)], pos_s.at[0], pos_r.at[0], up, wv),
        remote(own_pos, posw.at[pl.ds(2 * tiles, tiles)], pos_s.at[1], pos_r.at[1], down, wv),
    )

    def pair_of(i):
        j = wv * (32 // n_wave) + i
        total = jnp.int32(0)
        tile = jnp.int32(0)
        base = jnp.int32(0)
        for t in range(tiles):
            total = total + counts_ref[t]
            past = total <= j
            tile = tile + past.astype(jnp.int32)
            base = jnp.where(past, total, base)
        tile = jnp.minimum(tile, tiles - 1)
        slot = jnp.clip(j - base, 0, lists_ref.shape[1] - 1)
        return tile, jnp.clip(lists_ref[tile, slot], 0, 3 * tiles - 1)

    pairs = 32 // n_wave

    def build_pair(i, _):
        tile, source = pair_of(i)
        target_rows = posw[tiles + tile]
        source_cols = jnp.transpose(posw[source])
        offs = []
        for c, side in enumerate((float(n_space), SIDE_CROSS, SIDE_CROSS)):
            off = target_rows[c : c + 1] - source_cols[:, c : c + 1]
            offs.append(off - F32(side) * jnp.floor(off * F32(1.0 / side) + 0.5))
        square = offs[0] * offs[0] + offs[1] * offs[1] + offs[2] * offs[2]
        diagonal = lax.broadcasted_iota(jnp.int32, (TILE, TILE), 0) == lax.broadcasted_iota(
            jnp.int32, (TILE, TILE), 1
        )
        own = jnp.where(source == tiles + tile, F32(0.0), F32(1.0))
        keep = jnp.where(diagonal, own, F32(1.0))
        envelope = NEAR_AMP * jnp.exp(-square / NEAR_SQUARE) * keep
        scaled_env = envelope / NEAR_SQUARE
        for a in range(3):
            left = offs[a] * scaled_env
            for b in range(a, 3):
                block = left * offs[b]
                if a == b:
                    block = block + envelope
                high = block.astype(BF16)
                low = (block - high.astype(F32)).astype(BF16)
                for p, q in sorted({(a, b), (b, a)}):
                    at = (i, slice(p * TILE, (p + 1) * TILE), slice(q * TILE, (q + 1) * TILE))
                    bm_hi[at] = high
                    bm_lo[at] = low
        return 0

    def near_apply(k):
        near[...] = jnp.zeros_like(near)

        def one_pair(i, _):
            tile, source = pair_of(i)
            f = u[k][source]
            lhs = split_rows(jnp.concatenate([f[0:8], f[8:16], f[16:24]], axis=1))
            res = jnp.dot(lhs, bm_hi[i], preferred_element_type=F32) + jnp.dot(
                lhs, bm_lo[i], preferred_element_type=F32
            )
            res = res[0:8] + res[8:16]
            res = jnp.concatenate([res[:, c * TILE : (c + 1) * TILE] for c in range(3)], axis=0)
            for t in range(tiles):
                near[t] += jnp.where(tile == t, res, 0.0)
            return 0

        lax.fori_loop(0, pairs, one_pair, 0)

    my_y, my_x, my_c = lax.div(me, 8), lax.rem(lax.div(me, 2), 4), lax.rem(me, 2)
    far = {0: 0, 1: 1, 2: 2, 3: 1}
    steps = [(dy, dx, dc) for dy in range(4) for dx in range(4) for dc in range(2)]
    steps = sorted(steps, key=lambda d: -(10 * (far[d[0]] + far[d[1]]) + d[2]))[:-1]
    n_chips = n_space // 2
    my_chip = lax.div(me, 2)
    chip_steps = [(dy, dx) for dy in range(4) for dx in range(4)]
    chip_steps = sorted(chip_steps, key=lambda d: -(far[d[0]] + far[d[1]]))

    def chip_at(dy, dx):
        return lax.rem(my_y + dy, 4) * 4 + lax.rem(my_x + dx, 4)

    ring_order = [4, 3, 5, 2, 6, 1, 7]

    def send_space(src_of, dst, ssem, rsem):
        for dy, dx, dc in steps:
            peer = lax.rem(my_y + dy, 4) * 8 + lax.rem(my_x + dx, 4) * 2 + lax.rem(my_c + dc, 2)
            remote(src_of(peer), dst, ssem, rsem, peer, wv).start()

    def all_but_one(ref, count, ssem, rsem):
        some = ref.at[pl.ds(0, count)]
        return remote(some, some, ssem, rsem, up, wv)

    sent = []

    for k in range(DEGREE):
        groups = ((0, 1), (2, 3), (4, 5), (6,), (7,)) if k > 0 else ()
        for group in groups:
            for j in group:
                d = distance(j)
                if d > 0:
                    piece = u[k].at[tiles + tile_at(d)]
                    sem = n_wave - d
                    remote(piece, piece, wa_s.at[k - 1], wa_r.at[k - 1, sem], up, wv).wait_recv()
            x = [u[k][tiles + tile_at(distance(j))] for j in group]
            lhs = split_rows(jnp.concatenate(x, axis=1))
            rows = slice(group[0] * TILE, (group[-1] + 1) * TILE)
            for n in range(2 * waves // step):
                cols = slice(n * step, (n + 1) * step)
                c = jnp.dot(lhs, ph_hi[rows, cols], preferred_element_type=F32) + jnp.dot(
                    lhs, ph_lo[rows, cols], preferred_element_type=F32
                )
                if group[0] == 0:
                    cacc[:, cols] = c[0:24] + c[24:48]
                else:
                    cacc[:, cols] += c[0:24] + c[24:48]
        for n in range(waves // step):
            for half in range(2):
                c = cacc[:, half * waves + n * step : half * waves + (n + 1) * step]
                for q in range(step // TILE):
                    lanes = slice(q * TILE, (q + 1) * TILE)
                    at = slice(n * step + q * TILE, n * step + (q + 1) * TILE)
                    c0, c1, c2 = c[0:8, lanes], c[8:16, lanes], c[16:24, lanes]
                    d0 = ev[0, :, at] * c0 + ev[1, :, at] * c1
                    d1 = ev[2, :, at] * c0 + ev[3, :, at] * c1 + ev[4, :, at] * c2
                    chip = half * (waves // TILE) + n * (step // TILE) + q
                    for tangent, d in ((0, d0), (1, d1)):
                        sbuf[k, tangent * (2 * waves // TILE) + chip] = d
        if k == 0:
            pl.semaphore_wait(barrier, n_space - 1 + n_wave - 1)
        for dy, dx in chip_steps:
            peer = chip_at(dy, dx)

            def send(peer=peer):
                remote(
                    sbuf.at[k, peer], rs.at[k, me], rs_s.at[k], rs_r.at[k], 2 * peer + 1, wv
                ).start()

            if (dy, dx) == (0, 0):
                pl.when(my_c == 0)(send)
            else:
                send()

        for copy in (pos_copies if k == 0 else ()) + halo(k):
            copy.start()
        if k == 0:
            lax.fori_loop(0, waves // TILE, make_transposed, 0)

        @pl.when(my_c == 1)
        def _():
            all_but_one(rs.at[k], n_space - 1, rs_s.at[k], rs_r.at[k]).wait_recv()
            rs[k, me] = sbuf[k, my_chip]
            sums = [rs[k, s] + rs[k, s + 1] for s in range(0, n_space, 2)]
            while len(sums) > 1:
                sums = [sums[s] + sums[s + 1] for s in range(0, len(sums), 2)]
            agb[k, my_chip] = sums[0]
            for dy, dx in chip_steps:
                for c in (0, 1):
                    if (dy, dx, c) != (0, 0, 1):
                        own = agb.at[k, my_chip]
                        remote(
                            own, own, ag_s.at[k], ag_r.at[k], 2 * chip_at(dy, dx) + c, wv
                        ).start()

        if k > 0:
            total = jnp.zeros((8, TILE), F32)
            for t in range(tiles):
                v = u[k][tiles + t]
                v = v * v
                total = total + (v[0:8] + v[8:16] + v[16:24])
            lane_sum = jnp.sum(total, axis=1, keepdims=True)
            pick = lax.broadcasted_iota(jnp.int32, (8, TILE), 0) == lax.broadcasted_iota(
                jnp.int32, (8, TILE), 1
            )
            row = jnp.sum(jnp.where(pick, lane_sum, 0.0), axis=0, keepdims=True)
            nsrc[k - 1] = row
            nrecv[k - 1, me] = row
            send_space(
                lambda peer: nsrc.at[k - 1],
                nrecv.at[k - 1, me],
                norm_s.at[k - 1],
                norm_r.at[k - 1],
            )
            sent.append((nrecv.at[k - 1], n_space - 1, norm_s.at[k - 1], norm_r.at[k - 1]))

        if k == 0:
            for copy in pos_copies:
                copy.wait_recv()
            lax.fori_loop(0, pairs, build_pair, 0)
        for copy in halo(k):
            copy.wait_recv()
        near_apply(k)

        @pl.when(my_c == 0)
        def _():
            all_but_one(agb.at[k], n_chips, ag_s.at[k], ag_r.at[k]).wait_recv()

        @pl.when(my_c == 1)
        def _():
            all_but_one(agb.at[k], n_chips - 1, ag_s.at[k], ag_r.at[k]).wait_recv()


        rows = [[], [], []]
        for half in range(2):
            for n in range(waves // TILE):
                at = slice(n * TILE, (n + 1) * TILE)
                chip = half * (waves // TILE) + n
                d = []
                for tangent in range(2):
                    d.append(agb[k, tangent * (2 * waves // TILE) + chip])
                rows[0].append(ev[0, :, at] * d[0] + ev[2, :, at] * d[1])
                rows[1].append(ev[1, :, at] * d[0] + ev[3, :, at] * d[1])
                rows[2].append(ev[4, :, at] * d[1])
        lhs = split_rows(
            jnp.concatenate([jnp.concatenate(r, axis=1) for r in rows], axis=0)
        )
        back[...] = lhs

        def back_pair(i, _):
            pair = tiles // 2 - 1 - i
            v = jnp.dot(back[...], pt_hi[pair], preferred_element_type=F32) + jnp.dot(
                back[...], pt_lo[pair], preferred_element_type=F32
            )
            v = v[0:24] + v[24:48]

            def part(d, q):
                t = tile_at(d)
                vbuf[k, t] = v[:, q * TILE : (q + 1) * TILE] + near[t]
                return t

            def send(t):
                remote(vbuf.at[k, t], wr.at[k, wv], wr_s.at[k], wr_r.at[k], me, t).start()

            send(part(distance(2 * pair + 1), 1))
            t = part(distance(2 * pair), 0)

            @pl.when(pair > 0)
            def _():
                send(t)

            return 0

        lax.fori_loop(0, n_wave // 2, back_pair, 0)
        wr[k, wv] = vbuf[k, wv] + u[k][tiles + wv]
        sent.append((wr.at[k], n_wave - 1, wr_s.at[k], wr_r.at[k]))
        if k == DEGREE - 1:
            for j in range(2):
                all_but_one(nrecv.at[j], n_space - 1, norm_s.at[j], norm_r.at[j]).wait_recv()
            sums = []
            for j in range(2):
                total = nrecv[j, 0]
                for s in range(1, n_space):
                    total = total + nrecv[j, s]
                sums.append(total)
            ratio = jnp.max(sums[1] / (sums[0] + EPSILON), axis=1, keepdims=True)
            high = SAFETY * jnp.sqrt(jnp.broadcast_to(ratio, (8, TILE)))
            low = high / SPREAD
            nodes = DEGREE + 1
            angles = [(j + 0.5) * math.pi / nodes for j in range(nodes)]
            samples = [
                jnp.sqrt(0.5 * (high - low) * F32(math.cos(a)) + 0.5 * (high + low)) for a in angles
            ]
            coeffs = []
            for order in range(nodes):
                c = samples[0] * F32(math.cos(order * angles[0]))
                for j in range(1, nodes):
                    c = c + samples[j] * F32(math.cos(order * angles[j]))
                coeffs.append(c * F32((1.0 if order == 0 else 2.0) / nodes))
            bound_sum = high + low
            scale = 1.0 / (high - low)
        all_but_one(wr.at[k], n_wave - 1, wr_s.at[k], wr_r.at[k]).wait_recv()
        image = wr[k, 0]
        for w in range(1, n_wave):
            image = image + wr[k, w]

        if k < DEGREE - 1:
            own = u[k + 1].at[tiles + wv]
            u[k + 1][tiles + wv] = image
            whole = u[k + 1].at[pl.ds(tiles, tiles)]
        else:
            pieces = []
            for c in range(3):
                at = slice(c * 8, (c + 1) * 8)
                f = u[0][tiles + wv, at]
                u1 = u[1][tiles + wv, at]
                u2 = u[2][tiles + wv, at]
                u3 = image[at]
                t1 = (2.0 * u1 - bound_sum * f) * scale
                mt1 = (2.0 * u2 - bound_sum * u1) * scale
                mmt1 = (2.0 * u3 - bound_sum * u2) * scale
                t2 = 2.0 * (2.0 * mt1 - bound_sum * t1) * scale - f
                mt2 = 2.0 * (2.0 * mmt1 - bound_sum * mt1) * scale - u1
                t3 = 2.0 * (2.0 * mt2 - bound_sum * t2) * scale - t1
                pieces.append(coeffs[0] * f + coeffs[1] * t1 + coeffs[2] * t2 + coeffs[3] * t3)
            own = outb.at[wv]
            outb[wv] = jnp.concatenate(pieces, axis=0)
            whole = outb

        for d in ring_order:
            remote(own, own, wa_s.at[k], wa_r.at[k, d], me, tile_at(d)).start()
        sent.append((whole, n_wave - 1, wa_s.at[k], wa_r.at[k, 0]))

    out_ref[wv] = outb[wv]
    for d in (1, 7, 2, 6, 3, 5, 4):
        piece = outb.at[tile_at(d)]
        remote(piece, piece, wa_s.at[2], wa_r.at[2, n_wave - d], up, wv).wait_recv()
        out_ref[tile_at(d)] = outb[tile_at(d)]
    for k in range(DEGREE):

        @pl.when(my_c == 0)
        def _():
            all_but_one(sbuf.at[k], n_chips, rs_s.at[k], rs_r.at[k]).wait_send()

        @pl.when(my_c == 1)
        def _():
            all_but_one(sbuf.at[k], n_chips - 1, rs_s.at[k], rs_r.at[k]).wait_send()
            all_but_one(rs.at[k], n_space - 1, ag_s.at[k], ag_r.at[k]).wait_send()

    for ref, count, ssem, rsem in sent:
        all_but_one(ref, count, ssem, rsem).wait_send()
    for copy in pos_copies:
        copy.wait_send()
    for k in range(DEGREE):
        for copy in halo(k):
            copy.wait_send()


def body(n_space, n_wave, noise, positions, wave_index, tile_lists, tile_counts):
    tiles = positions.shape[1] // TILE
    count = positions.shape[1]
    waves = wave_index.shape[1]
    vectors = noise.shape[0]
    rows = vectors * 3
    arranged = jnp.transpose(noise, (1, 0, 2)).reshape(rows, count)
    pairs = 32 // n_wave
    vmem = pl.BlockSpec(memory_space=pltpu.VMEM)
    dma = pltpu.SemaphoreType.DMA

    hbm = pl.BlockSpec(memory_space=pl.ANY)
    out = pl.pallas_call(
        functools.partial(kernel, n_space, n_wave),
        out_shape=jax.ShapeDtypeStruct((tiles, rows, TILE), F32),
        in_specs=[hbm] * 5,
        out_specs=vmem,
        scratch_shapes=[
            pltpu.VMEM((3, count), F32),
            pltpu.VMEM((3, waves), jnp.int32),
            pltpu.SMEM(tile_lists.shape, jnp.int32),
            pltpu.SMEM(tile_counts.shape, jnp.int32),
            pltpu.VMEM((rows, 2 * waves), F32),
            pltpu.VMEM((2 * rows, 2 * waves), BF16),
            pltpu.VMEM((count, 2 * waves), BF16),
            pltpu.VMEM((count, 2 * waves), BF16),
            pltpu.VMEM((tiles // 2, 2 * waves, 2 * TILE), BF16),
            pltpu.VMEM((tiles // 2, 2 * waves, 2 * TILE), BF16),
            pltpu.VMEM((3 * tiles, 8, TILE), F32),
            pltpu.VMEM((5, 8, waves), F32),
            pltpu.VMEM((24, waves), BF16),
            pltpu.VMEM((waves, 24), BF16),
            pltpu.VMEM((24, count), BF16),
            pltpu.VMEM((TILE, waves), F32),
            pltpu.VMEM((TILE, count), F32),
            pltpu.VMEM((pairs, 3 * TILE, 3 * TILE), BF16),
            pltpu.VMEM((pairs, 3 * TILE, 3 * TILE), BF16),
            pltpu.VMEM((3 * tiles, rows, TILE), F32),
            pltpu.VMEM((3 * tiles, rows, TILE), F32),
            pltpu.VMEM((3 * tiles, rows, TILE), F32),
            pltpu.VMEM((tiles, rows, TILE), F32),
            pltpu.VMEM((DEGREE, n_space // 2, 8, TILE), F32),
            pltpu.VMEM((DEGREE, n_space, 8, TILE), F32),
            pltpu.VMEM((DEGREE, n_space // 2, 8, TILE), F32),
            pltpu.VMEM((DEGREE, tiles, rows, TILE), F32),
            pltpu.VMEM((DEGREE, tiles, rows, TILE), F32),
            pltpu.VMEM((2, 1, TILE), F32),
            pltpu.VMEM((2, n_space, 1, TILE), F32),
            pltpu.VMEM((tiles, rows, TILE), F32),
            dma((DEGREE,)),
            dma((DEGREE,)),
            dma((DEGREE,)),
            dma((DEGREE,)),
            dma((DEGREE,)),
            dma((DEGREE,)),
            dma((DEGREE,)),
            dma((DEGREE, n_wave)),
            dma((DEGREE, 2)),
            dma((DEGREE, 2)),
            dma((2,)),
            dma((2,)),
            dma((2,)),
            dma((2,)),
            dma((4 + tiles,)),
        ],
        compiler_params=pltpu.CompilerParams(
            collective_id=0, has_side_effects=True, vmem_limit_bytes=60 * 1024 * 1024
        ),
    )(arranged, positions, wave_index, tile_lists, tile_counts)
    out = out.reshape(tiles, 3, vectors, TILE)
    return jnp.transpose(out, (2, 1, 0, 3)).reshape(vectors, 3, count)


def solution(mesh):
    n_space, n_wave = mesh.shape["space"], mesh.shape["wave"]

    def step(*args):
        return body(n_space, n_wave, *args)

    in_specs = (
        P(None, None, "space"),
        P(None, "space"),
        P(None, "wave"),
        P("space", None),
        P("space"),
    )
    out_specs = P(None, None, "space")
    return jax.shard_map(step, mesh=mesh, in_specs=in_specs, out_specs=out_specs, check_vma=False)
```

```python
import functools
import math

import jax
import jax.numpy as jnp
from jax import lax
from jax.experimental import pallas as pl
from jax.experimental.pallas import tpu as pltpu
from jax.sharding import PartitionSpec as P

MESH = pl.DeviceIdType.MESH
F32 = jnp.float32
BF16 = jnp.bfloat16

KW = 4096
DEGREE = 3
TILE = 128
SIDE_CROSS = 8.0
NEAR_SQUARE = 0.36
NEAR_AMP = 0.15
FAR_AMP = 8.0
SPLIT_SQUARE = 64.0
SCREEN = 4.0
SAFETY = 1.25
SPREAD = 100.0
EPSILON = 1e-06

ODD = (4.442882834148948, -7.308241154482914, 3.6062889571583123, -0.8457635896353835, 0.10920574060672703)
EVEN = (1.4142134965574307, -6.978850987759868, 5.7394611627073875, -1.8835629390376682, 0.31069809581455876)


def split_rows(x):
    high = x.astype(BF16).astype(F32)
    return jnp.concatenate([high, x - high], axis=0).astype(BF16)


def nearest(x):
    return lax.round(x, lax.RoundingMethod.TO_NEAREST_EVEN)


def polynomial(coeffs, x):
    p = F32(coeffs[-1])
    for c in coeffs[-2::-1]:
        p = p * x + F32(c)
    return p


def kernel(
    n_space,
    n_wave,
    noise_hbm,
    pos_hbm,
    wave_hbm,
    lists_hbm,
    counts_hbm,
    out_ref,
    pos_ref,
    wave_ref,
    lists_ref,
    counts_ref,
    cacc,
    back,
    ph_hi,
    ph_lo,
    pt_hi,
    pt_lo,
    posw,
    ev,
    nf,
    nt,
    pf,
    turns,
    turns_t,
    bm_hi,
    bm_lo,
    u0,
    u1_,
    u2_,
    near,
    sbuf,
    rs,
    agb,
    vbuf,
    wr,
    nsrc,
    nrecv,
    outb,
    rs_s,
    rs_r,
    ag_s,
    ag_r,
    wr_s,
    wr_r,
    wa_s,
    wa_r,
    halo_s,
    halo_r,
    pos_s,
    pos_r,
    norm_s,
    norm_r,
    in_s,
):
    me = lax.axis_index("space")
    wv = lax.axis_index("wave")
    up = lax.rem(me + 1, n_space)
    down = lax.rem(me + n_space - 1, n_space)
    tiles = n_wave
    u = (u0, u1_, u2_)

    loads = [
        pltpu.make_async_copy(pos_hbm, pos_ref, in_s.at[0]),
        pltpu.make_async_copy(wave_hbm, wave_ref, in_s.at[1]),
    ]
    for t in range(tiles):
        loads.append(
            pltpu.make_async_copy(
                noise_hbm.at[:, pl.ds(t * TILE, TILE)], u[0].at[tiles + t], in_s.at[4 + t]
            )
        )
    loads.append(pltpu.make_async_copy(lists_hbm, lists_ref, in_s.at[2]))
    loads.append(pltpu.make_async_copy(counts_hbm, counts_ref, in_s.at[3]))
    for copy in loads:
        copy.start()

    barrier = pltpu.get_barrier_semaphore()

    def greet_space(d, _):
        pl.semaphore_signal(
            barrier, inc=1, device_id=(lax.rem(me + d, n_space), wv), device_id_type=MESH
        )
        return 0

    def greet_wave(d, _):
        pl.semaphore_signal(
            barrier, inc=1, device_id=(me, lax.rem(wv + d, n_wave)), device_id_type=MESH
        )
        return 0

    lax.fori_loop(1, n_space, greet_space, 0)
    lax.fori_loop(1, n_wave, greet_wave, 0)

    def remote(src, dst, ssem, rsem, s, w):
        return pltpu.make_async_remote_copy(
            src_ref=src,
            dst_ref=dst,
            send_sem=ssem,
            recv_sem=rsem,
            device_id=(s, w),
            device_id_type=MESH,
        )

    for copy in loads[:2]:
        copy.wait()

    for t in range(tiles):
        lanes = slice(t * TILE, (t + 1) * TILE)
        posw[tiles + t] = jnp.concatenate(
            [pos_ref[:, lanes], jnp.zeros((5, TILE), F32)], axis=0
        )

    waves = wave_ref.shape[1]
    n_all = wave_ref[...].astype(F32)
    n_rows = [jnp.broadcast_to(n_all[c : c + 1], (8, waves)) for c in range(3)]
    ka = n_rows[0] * F32(2.0 * math.pi / n_space)
    kb = n_rows[1] * F32(2.0 * math.pi / SIDE_CROSS)
    kc = n_rows[2] * F32(2.0 * math.pi / SIDE_CROSS)
    plane = ka * ka + kb * kb
    square = plane + kc * kc
    scaled = square / SPLIT_SQUARE
    weight = FAR_AMP * (1.0 + scaled) * jnp.exp(-scaled) / (KW * (square + SCREEN))
    root = jnp.sqrt(weight)
    rho = jnp.sqrt(plane)
    length = jnp.sqrt(square)
    ev[0] = -root * kb / rho
    ev[1] = root * ka / rho
    ev[2] = -root * ka * kc / (rho * length)
    ev[3] = -root * kb * kc / (rho * length)
    ev[4] = root * rho / length
    padded = jnp.concatenate([n_all, jnp.zeros((5, waves), F32)], axis=0)
    padded = jnp.concatenate([padded] * 3, axis=0)
    nf[...] = padded.astype(BF16)
    for n in range(waves // TILE):
        at = slice(n * TILE, (n + 1) * TILE)
        nt[at, :] = jnp.transpose(padded[:, at]).astype(BF16)
    sides = jnp.where(
        lax.broadcasted_iota(jnp.int32, (8, TILE), 0) == 0, F32(1.0 / n_space), F32(1.0 / SIDE_CROSS)
    )

    def trig(angle):
        r = angle - nearest(angle)
        r2 = r * r
        half_sine = polynomial(ODD, r2) * r
        cosine = 1.0 - half_sine * half_sine
        sine = half_sine * polynomial(EVEN, r2)
        halves = []
        for value in (cosine, sine):
            high = value.astype(BF16)
            halves.append((high, (value - high.astype(F32)).astype(BF16)))
        return halves

    def tile_at(d):
        return lax.rem(wv + d, n_wave)

    def distance(j):
        if isinstance(j, int):
            return (j + 1) // 2 if j % 2 == 1 else (n_wave - j // 2) % n_wave
        half = lax.div(j + 1, 2)
        return jnp.where(lax.rem(j, 2) == 1, half, lax.rem(n_wave - half, n_wave))

    def make_phases(t):
        box = posw[tiles + tile_at(distance(t))] * sides
        first = box.astype(BF16).astype(F32)
        second = (box - first).astype(BF16).astype(F32)
        pieces = jnp.concatenate([first, second, box - first - second], axis=0)
        pf[:, pl.ds(pl.multiple_of(t * TILE, TILE), TILE)] = pieces.astype(BF16)
        turns[...] = jnp.dot(
            jnp.transpose(pieces).astype(BF16), nf[...], preferred_element_type=F32
        )
        for j in range(TILE // 16):
            rows = pl.ds(pl.multiple_of(t * TILE + j * 16, 16), 16)
            for at, (high, low) in zip((0, waves), trig(turns[j * 16 : (j + 1) * 16])):
                ph_hi[rows, at : at + waves] = high
                ph_lo[rows, at : at + waves] = low

    def make_transposed(n, _):
        block = nt[pl.ds(pl.multiple_of(n * TILE, TILE), TILE), :]
        turns_t[...] = jnp.dot(block, pf[...], preferred_element_type=F32)
        for j in range(TILE // 16):
            for pair in range(tiles // 2):
                lanes = slice(pair * 2 * TILE, (pair + 1) * 2 * TILE)
                parts = trig(turns_t[j * 16 : (j + 1) * 16, lanes])
                for at, (high, low) in zip((0, waves), parts):
                    rows = pl.ds(pl.multiple_of(at + n * TILE + j * 16, 16), 16)
                    pt_hi[pair, rows, :] = high
                    pt_lo[pair, rows, :] = low
        return 0

    step = 256

    def fold(t):
        lhs = split_rows(u[0][tiles + tile_at(distance(t))])
        rows = pl.ds(pl.multiple_of(t * TILE, TILE), TILE)
        for n in range(2 * waves // step):
            cols = slice(n * step, (n + 1) * step)
            c = jnp.dot(lhs, ph_hi[rows, cols], preferred_element_type=F32) + jnp.dot(
                lhs, ph_lo[rows, cols], preferred_element_type=F32
            )
            cacc[:, cols] += c[0:24] + c[24:48]

    def fold_and_make(t, _):
        fold(t - 1)
        make_phases(t)
        return 0

    cacc[...] = jnp.zeros_like(cacc)
    make_phases(0)
    for copy in loads[2:]:
        copy.wait()
    lax.fori_loop(1, tiles, fold_and_make, 0)
    fold(tiles - 1)

    def halo(k):
        own = u[k].at[pl.ds(tiles, tiles)]
        return (
            remote(own, u[k].at[pl.ds(0, tiles)], halo_s.at[k, 0], halo_r.at[k, 0], up, wv),
            remote(own, u[k].at[pl.ds(2 * tiles, tiles)], halo_s.at[k, 1], halo_r.at[k, 1], down, wv),
        )

    own_pos = posw.at[pl.ds(tiles, tiles)]
    pos_copies = (
        remote(own_pos, posw.at[pl.ds(0, tiles)], pos_s.at[0], pos_r.at[0], up, wv),
        remote(own_pos, posw.at[pl.ds(2 * tiles, tiles)], pos_s.at[1], pos_r.at[1], down, wv),
    )

    def pair_of(i):
        j = wv * (32 // n_wave) + i
        total = jnp.int32(0)
        tile = jnp.int32(0)
        base = jnp.int32(0)
        for t in range(tiles):
            total = total + counts_ref[t]
            past = total <= j
            tile = tile + past.astype(jnp.int32)
            base = jnp.where(past, total, base)
        tile = jnp.minimum(tile, tiles - 1)
        slot = jnp.clip(j - base, 0, lists_ref.shape[1] - 1)
        return tile, jnp.clip(lists_ref[tile, slot], 0, 3 * tiles - 1)

    pairs = 32 // n_wave

    def build_pair(i, _):
        tile, source = pair_of(i)
        target_rows = posw[tiles + tile]
        source_cols = jnp.transpose(posw[source])
        offs = []
        for c, side in enumerate((float(n_space), SIDE_CROSS, SIDE_CROSS)):
            off = target_rows[c : c + 1] - source_cols[:, c : c + 1]
            offs.append(off - F32(side) * jnp.floor(off * F32(1.0 / side) + 0.5))
        square = offs[0] * offs[0] + offs[1] * offs[1] + offs[2] * offs[2]
        diagonal = lax.broadcasted_iota(jnp.int32, (TILE, TILE), 0) == lax.broadcasted_iota(
            jnp.int32, (TILE, TILE), 1
        )
        own = jnp.where(source == tiles + tile, F32(0.0), F32(1.0))
        keep = jnp.where(diagonal, own, F32(1.0))
        envelope = NEAR_AMP * jnp.exp(-square / NEAR_SQUARE) * keep
        scaled_env = envelope / NEAR_SQUARE
        for a in range(3):
            left = offs[a] * scaled_env
            for b in range(a, 3):
                block = left * offs[b]
                if a == b:
                    block = block + envelope
                high = block.astype(BF16)
                low = (block - high.astype(F32)).astype(BF16)
                for p, q in sorted({(a, b), (b, a)}):
                    at = (i, slice(p * TILE, (p + 1) * TILE), slice(q * TILE, (q + 1) * TILE))
                    bm_hi[at] = high
                    bm_lo[at] = low
        return 0

    def near_apply(k):
        near[...] = jnp.zeros_like(near)

        def one_pair(i, _):
            tile, source = pair_of(i)
            f = u[k][source]
            lhs = split_rows(jnp.concatenate([f[0:8], f[8:16], f[16:24]], axis=1))
            res = jnp.dot(lhs, bm_hi[i], preferred_element_type=F32) + jnp.dot(
                lhs, bm_lo[i], preferred_element_type=F32
            )
            res = res[0:8] + res[8:16]
            res = jnp.concatenate([res[:, c * TILE : (c + 1) * TILE] for c in range(3)], axis=0)
            for t in range(tiles):
                near[t] += jnp.where(tile == t, res, 0.0)
            return 0

        lax.fori_loop(0, pairs, one_pair, 0)

    my_y, my_x, my_c = lax.div(me, 8), lax.rem(lax.div(me, 2), 4), lax.rem(me, 2)
    far = {0: 0, 1: 1, 2: 2, 3: 1}
    steps = [(dy, dx, dc) for dy in range(4) for dx in range(4) for dc in range(2)]
    steps = sorted(steps, key=lambda d: -(10 * (far[d[0]] + far[d[1]]) + d[2]))[:-1]
    n_chips = n_space // 2
    my_chip = lax.div(me, 2)
    chip_steps = [(dy, dx) for dy in range(4) for dx in range(4)]
    chip_steps = sorted(chip_steps, key=lambda d: -(far[d[0]] + far[d[1]]))

    def chip_at(dy, dx):
        return lax.rem(my_y + dy, 4) * 4 + lax.rem(my_x + dx, 4)

    ring_order = [4, 3, 5, 2, 6, 1, 7]

    def send_space(src_of, dst, ssem, rsem):
        for dy, dx, dc in steps:
            peer = lax.rem(my_y + dy, 4) * 8 + lax.rem(my_x + dx, 4) * 2 + lax.rem(my_c + dc, 2)
            remote(src_of(peer), dst, ssem, rsem, peer, wv).start()

    def all_but_one(ref, count, ssem, rsem):
        some = ref.at[pl.ds(0, count)]
        return remote(some, some, ssem, rsem, up, wv)

    sent = []

    for k in range(DEGREE):
        groups = ((0, 1), (2, 3), (4, 5), (6,), (7,)) if k > 0 else ()
        for group in groups:
            for j in group:
                d = distance(j)
                if d > 0:
                    piece = u[k].at[tiles + tile_at(d)]
                    sem = n_wave - d
                    remote(piece, piece, wa_s.at[k - 1], wa_r.at[k - 1, sem], up, wv).wait_recv()
            x = [u[k][tiles + tile_at(distance(j))] for j in group]
            lhs = split_rows(jnp.concatenate(x, axis=1))
            rows = slice(group[0] * TILE, (group[-1] + 1) * TILE)
            for n in range(2 * waves // step):
                cols = slice(n * step, (n + 1) * step)
                c = jnp.dot(lhs, ph_hi[rows, cols], preferred_element_type=F32) + jnp.dot(
                    lhs, ph_lo[rows, cols], preferred_element_type=F32
                )
                if group[0] == 0:
                    cacc[:, cols] = c[0:24] + c[24:48]
                else:
                    cacc[:, cols] += c[0:24] + c[24:48]
        for n in range(waves // step):
            for half in range(2):
                c = cacc[:, half * waves + n * step : half * waves + (n + 1) * step]
                for q in range(step // TILE):
                    lanes = slice(q * TILE, (q + 1) * TILE)
                    at = slice(n * step + q * TILE, n * step + (q + 1) * TILE)
                    c0, c1, c2 = c[0:8, lanes], c[8:16, lanes], c[16:24, lanes]
                    d0 = ev[0, :, at] * c0 + ev[1, :, at] * c1
                    d1 = ev[2, :, at] * c0 + ev[3, :, at] * c1 + ev[4, :, at] * c2
                    chip = half * (waves // TILE) + n * (step // TILE) + q
                    for tangent, d in ((0, d0), (1, d1)):
                        sbuf[k, tangent * (2 * waves // TILE) + chip] = d
        if k == 0:
            pl.semaphore_wait(barrier, n_space - 1 + n_wave - 1)
        for dy, dx in chip_steps:
            peer = chip_at(dy, dx)

            def send(peer=peer):
                remote(
                    sbuf.at[k, peer], rs.at[k, me], rs_s.at[k], rs_r.at[k], 2 * peer + 1, wv
                ).start()

            if (dy, dx) == (0, 0):
                pl.when(my_c == 0)(send)
            else:
                send()

        for copy in (pos_copies if k == 0 else ()) + halo(k):
            copy.start()
        if k == 0:
            lax.fori_loop(0, waves // TILE, make_transposed, 0)

        @pl.when(my_c == 1)
        def _():
            all_but_one(rs.at[k], n_space - 1, rs_s.at[k], rs_r.at[k]).wait_recv()
            rs[k, me] = sbuf[k, my_chip]
            sums = [rs[k, s] + rs[k, s + 1] for s in range(0, n_space, 2)]
            while len(sums) > 1:
                sums = [sums[s] + sums[s + 1] for s in range(0, len(sums), 2)]
            agb[k, my_chip] = sums[0]
            for dy, dx in chip_steps:
                for c in (0, 1):
                    if (dy, dx, c) != (0, 0, 1):
                        own = agb.at[k, my_chip]
                        remote(
                            own, own, ag_s.at[k], ag_r.at[k], 2 * chip_at(dy, dx) + c, wv
                        ).start()

        if k > 0:
            total = jnp.zeros((8, TILE), F32)
            for t in range(tiles):
                v = u[k][tiles + t]
                v = v * v
                total = total + (v[0:8] + v[8:16] + v[16:24])
            lane_sum = jnp.sum(total, axis=1, keepdims=True)
            pick = lax.broadcasted_iota(jnp.int32, (8, TILE), 0) == lax.broadcasted_iota(
                jnp.int32, (8, TILE), 1
            )
            row = jnp.sum(jnp.where(pick, lane_sum, 0.0), axis=0, keepdims=True)
            nsrc[k - 1] = row
            nrecv[k - 1, me] = row
            send_space(
                lambda peer: nsrc.at[k - 1],
                nrecv.at[k - 1, me],
                norm_s.at[k - 1],
                norm_r.at[k - 1],
            )
            sent.append((nrecv.at[k - 1], n_space - 1, norm_s.at[k - 1], norm_r.at[k - 1]))

        if k == 0:
            for copy in pos_copies:
                copy.wait_recv()
            lax.fori_loop(0, pairs, build_pair, 0)
        for copy in halo(k):
            copy.wait_recv()
        near_apply(k)

        @pl.when(my_c == 0)
        def _():
            all_but_one(agb.at[k], n_chips, ag_s.at[k], ag_r.at[k]).wait_recv()

        @pl.when(my_c == 1)
        def _():
            all_but_one(agb.at[k], n_chips - 1, ag_s.at[k], ag_r.at[k]).wait_recv()


        rows = [[], [], []]
        for half in range(2):
            for n in range(waves // TILE):
                at = slice(n * TILE, (n + 1) * TILE)
                chip = half * (waves // TILE) + n
                d = []
                for tangent in range(2):
                    d.append(agb[k, tangent * (2 * waves // TILE) + chip])
                rows[0].append(ev[0, :, at] * d[0] + ev[2, :, at] * d[1])
                rows[1].append(ev[1, :, at] * d[0] + ev[3, :, at] * d[1])
                rows[2].append(ev[4, :, at] * d[1])
        lhs = split_rows(
            jnp.concatenate([jnp.concatenate(r, axis=1) for r in rows], axis=0)
        )
        back[...] = lhs

        def back_pair(i, _):
            pair = tiles // 2 - 1 - i
            v = jnp.dot(back[...], pt_hi[pair], preferred_element_type=F32) + jnp.dot(
                back[...], pt_lo[pair], preferred_element_type=F32
            )
            v = v[0:24] + v[24:48]

            def part(d, q):
                t = tile_at(d)
                vbuf[k, t] = v[:, q * TILE : (q + 1) * TILE] + near[t]
                return t

            def send(t):
                remote(vbuf.at[k, t], wr.at[k, wv], wr_s.at[k], wr_r.at[k], me, t).start()

            send(part(distance(2 * pair + 1), 1))
            t = part(distance(2 * pair), 0)

            @pl.when(pair > 0)
            def _():
                send(t)

            return 0

        lax.fori_loop(0, n_wave // 2, back_pair, 0)
        wr[k, wv] = vbuf[k, wv] + u[k][tiles + wv]
        sent.append((wr.at[k], n_wave - 1, wr_s.at[k], wr_r.at[k]))
        if k == DEGREE - 1:
            for j in range(2):
                all_but_one(nrecv.at[j], n_space - 1, norm_s.at[j], norm_r.at[j]).wait_recv()
            sums = []
            for j in range(2):
                total = nrecv[j, 0]
                for s in range(1, n_space):
                    total = total + nrecv[j, s]
                sums.append(total)
            ratio = jnp.max(sums[1] / (sums[0] + EPSILON), axis=1, keepdims=True)
            high = SAFETY * jnp.sqrt(jnp.broadcast_to(ratio, (8, TILE)))
            low = high / SPREAD
            nodes = DEGREE + 1
            angles = [(j + 0.5) * math.pi / nodes for j in range(nodes)]
            samples = [
                jnp.sqrt(0.5 * (high - low) * F32(math.cos(a)) + 0.5 * (high + low)) for a in angles
            ]
            coeffs = []
            for order in range(nodes):
                c = samples[0] * F32(math.cos(order * angles[0]))
                for j in range(1, nodes):
                    c = c + samples[j] * F32(math.cos(order * angles[j]))
                coeffs.append(c * F32((1.0 if order == 0 else 2.0) / nodes))
            bound_sum = high + low
            scale = 1.0 / (high - low)
        all_but_one(wr.at[k], n_wave - 1, wr_s.at[k], wr_r.at[k]).wait_recv()
        image = wr[k, 0]
        for w in range(1, n_wave):
            image = image + wr[k, w]

        if k < DEGREE - 1:
            own = u[k + 1].at[tiles + wv]
            u[k + 1][tiles + wv] = image
            whole = u[k + 1].at[pl.ds(tiles, tiles)]
        else:
            pieces = []
            for c in range(3):
                at = slice(c * 8, (c + 1) * 8)
                f = u[0][tiles + wv, at]
                u1 = u[1][tiles + wv, at]
                u2 = u[2][tiles + wv, at]
                u3 = image[at]
                t1 = (2.0 * u1 - bound_sum * f) * scale
                mt1 = (2.0 * u2 - bound_sum * u1) * scale
                mmt1 = (2.0 * u3 - bound_sum * u2) * scale
                t2 = 2.0 * (2.0 * mt1 - bound_sum * t1) * scale - f
                mt2 = 2.0 * (2.0 * mmt1 - bound_sum * mt1) * scale - u1
                t3 = 2.0 * (2.0 * mt2 - bound_sum * t2) * scale - t1
                pieces.append(coeffs[0] * f + coeffs[1] * t1 + coeffs[2] * t2 + coeffs[3] * t3)
            own = outb.at[wv]
            outb[wv] = jnp.concatenate(pieces, axis=0)
            whole = outb

        for d in ring_order:
            remote(own, own, wa_s.at[k], wa_r.at[k, d], me, tile_at(d)).start()
        sent.append((whole, n_wave - 1, wa_s.at[k], wa_r.at[k, 0]))

    def put(t):
        out_ref[:, pl.ds(pl.multiple_of(t * TILE, TILE), TILE)] = outb[t]

    put(wv)
    for d in (1, 7, 2, 6, 3, 5, 4):
        piece = outb.at[tile_at(d)]
        remote(piece, piece, wa_s.at[2], wa_r.at[2, n_wave - d], up, wv).wait_recv()
        put(tile_at(d))
    for k in range(DEGREE):

        @pl.when(my_c == 0)
        def _():
            all_but_one(sbuf.at[k], n_chips, rs_s.at[k], rs_r.at[k]).wait_send()

        @pl.when(my_c == 1)
        def _():
            all_but_one(sbuf.at[k], n_chips - 1, rs_s.at[k], rs_r.at[k]).wait_send()
            all_but_one(rs.at[k], n_space - 1, ag_s.at[k], ag_r.at[k]).wait_send()

    for ref, count, ssem, rsem in sent:
        all_but_one(ref, count, ssem, rsem).wait_send()
    for copy in pos_copies:
        copy.wait_send()
    for k in range(DEGREE):
        for copy in halo(k):
            copy.wait_send()


def body(n_space, n_wave, noise, positions, wave_index, tile_lists, tile_counts):
    tiles = positions.shape[1] // TILE
    count = positions.shape[1]
    waves = wave_index.shape[1]
    vectors = noise.shape[0]
    rows = vectors * 3
    arranged = jnp.transpose(noise, (1, 0, 2)).reshape(rows, count)
    pairs = 32 // n_wave
    vmem = pl.BlockSpec(memory_space=pltpu.VMEM)
    dma = pltpu.SemaphoreType.DMA

    hbm = pl.BlockSpec(memory_space=pl.ANY)
    out = pl.pallas_call(
        functools.partial(kernel, n_space, n_wave),
        out_shape=pltpu.VMEM((rows, count), F32),
        in_specs=[hbm] * 5,
        out_specs=vmem,
        scratch_shapes=[
            pltpu.VMEM((3, count), F32),
            pltpu.VMEM((3, waves), jnp.int32),
            pltpu.SMEM(tile_lists.shape, jnp.int32),
            pltpu.SMEM(tile_counts.shape, jnp.int32),
            pltpu.VMEM((rows, 2 * waves), F32),
            pltpu.VMEM((2 * rows, 2 * waves), BF16),
            pltpu.VMEM((count, 2 * waves), BF16),
            pltpu.VMEM((count, 2 * waves), BF16),
            pltpu.VMEM((tiles // 2, 2 * waves, 2 * TILE), BF16),
            pltpu.VMEM((tiles // 2, 2 * waves, 2 * TILE), BF16),
            pltpu.VMEM((3 * tiles, 8, TILE), F32),
            pltpu.VMEM((5, 8, waves), F32),
            pltpu.VMEM((24, waves), BF16),
            pltpu.VMEM((waves, 24), BF16),
            pltpu.VMEM((24, count), BF16),
            pltpu.VMEM((TILE, waves), F32),
            pltpu.VMEM((TILE, count), F32),
            pltpu.VMEM((pairs, 3 * TILE, 3 * TILE), BF16),
            pltpu.VMEM((pairs, 3 * TILE, 3 * TILE), BF16),
            pltpu.VMEM((3 * tiles, rows, TILE), F32),
            pltpu.VMEM((3 * tiles, rows, TILE), F32),
            pltpu.VMEM((3 * tiles, rows, TILE), F32),
            pltpu.VMEM((tiles, rows, TILE), F32),
            pltpu.VMEM((DEGREE, n_space // 2, 8, TILE), F32),
            pltpu.VMEM((DEGREE, n_space, 8, TILE), F32),
            pltpu.VMEM((DEGREE, n_space // 2, 8, TILE), F32),
            pltpu.VMEM((DEGREE, tiles, rows, TILE), F32),
            pltpu.VMEM((DEGREE, tiles, rows, TILE), F32),
            pltpu.VMEM((2, 1, TILE), F32),
            pltpu.VMEM((2, n_space, 1, TILE), F32),
            pltpu.VMEM((tiles, rows, TILE), F32),
            dma((DEGREE,)),
            dma((DEGREE,)),
            dma((DEGREE,)),
            dma((DEGREE,)),
            dma((DEGREE,)),
            dma((DEGREE,)),
            dma((DEGREE,)),
            dma((DEGREE, n_wave)),
            dma((DEGREE, 2)),
            dma((DEGREE, 2)),
            dma((2,)),
            dma((2,)),
            dma((2,)),
            dma((2,)),
            dma((4 + tiles,)),
        ],
        compiler_params=pltpu.CompilerParams(
            collective_id=0, has_side_effects=True, vmem_limit_bytes=60 * 1024 * 1024
        ),
    )(arranged, positions, wave_index, tile_lists, tile_counts)
    return jnp.transpose(out.reshape(3, vectors, count), (1, 0, 2))


def solution(mesh):
    n_space, n_wave = mesh.shape["space"], mesh.shape["wave"]

    def step(*args):
        return body(n_space, n_wave, *args)

    in_specs = (
        P(None, None, "space"),
        P(None, "space"),
        P(None, "wave"),
        P("space", None),
        P("space"),
    )
    out_specs = P(None, None, "space")
    return jax.shard_map(step, mesh=mesh, in_specs=in_specs, out_specs=out_specs, check_vma=False)
```

```python
import functools
import math

import jax
import jax.numpy as jnp
from jax import lax
from jax.experimental import pallas as pl
from jax.experimental.pallas import tpu as pltpu
from jax.sharding import PartitionSpec as P

MESH = pl.DeviceIdType.MESH
F32 = jnp.float32
BF16 = jnp.bfloat16

KW = 4096
DEGREE = 3
TILE = 128
SIDE_CROSS = 8.0
NEAR_SQUARE = 0.36
NEAR_AMP = 0.15
FAR_AMP = 8.0
SPLIT_SQUARE = 64.0
SCREEN = 4.0
SAFETY = 1.25
SPREAD = 100.0
EPSILON = 1e-06

ODD = (4.442882834148948, -7.308241154482914, 3.6062889571583123, -0.8457635896353835, 0.10920574060672703)
EVEN = (1.4142134965574307, -6.978850987759868, 5.7394611627073875, -1.8835629390376682, 0.31069809581455876)


def split_rows(x):
    high = x.astype(BF16).astype(F32)
    return jnp.concatenate([high, x - high], axis=0).astype(BF16)


def nearest(x):
    return lax.round(x, lax.RoundingMethod.TO_NEAREST_EVEN)


def polynomial(coeffs, x):
    p = F32(coeffs[-1])
    for c in coeffs[-2::-1]:
        p = p * x + F32(c)
    return p


def kernel(
    n_space,
    n_wave,
    noise_hbm,
    pos_hbm,
    wave_hbm,
    lists_hbm,
    counts_hbm,
    out_ref,
    pos_ref,
    wave_ref,
    lists_ref,
    counts_ref,
    cacc,
    back,
    ph_hi,
    ph_lo,
    pt_hi,
    pt_lo,
    posw,
    ev,
    nf,
    nt,
    pf,
    turns,
    turns_t,
    bm_hi,
    bm_lo,
    u0,
    u1_,
    u2_,
    near,
    sbuf,
    rs,
    agb,
    vbuf,
    wr,
    nsrc,
    nrecv,
    outb,
    rs_s,
    rs_r,
    ag_s,
    ag_r,
    wr_s,
    wr_r,
    wa_s,
    wa_r,
    halo_s,
    halo_r,
    pos_s,
    pos_r,
    norm_s,
    norm_r,
    in_s,
):
    me = lax.axis_index("space")
    wv = lax.axis_index("wave")
    up = lax.rem(me + 1, n_space)
    down = lax.rem(me + n_space - 1, n_space)
    tiles = n_wave
    u = (u0, u1_, u2_)

    loads = [
        pltpu.make_async_copy(pos_hbm, pos_ref, in_s.at[0]),
        pltpu.make_async_copy(wave_hbm, wave_ref, in_s.at[1]),
    ]
    for t in range(tiles):
        loads.append(
            pltpu.make_async_copy(
                noise_hbm.at[:, pl.ds(t * TILE, TILE)], u[0].at[tiles + t], in_s.at[4 + t]
            )
        )
    loads.append(pltpu.make_async_copy(lists_hbm, lists_ref, in_s.at[2]))
    loads.append(pltpu.make_async_copy(counts_hbm, counts_ref, in_s.at[3]))
    for copy in loads:
        copy.start()

    barrier = pltpu.get_barrier_semaphore()

    def greet_space(d, _):
        pl.semaphore_signal(
            barrier, inc=1, device_id=(lax.rem(me + d, n_space), wv), device_id_type=MESH
        )
        return 0

    def greet_wave(d, _):
        pl.semaphore_signal(
            barrier, inc=1, device_id=(me, lax.rem(wv + d, n_wave)), device_id_type=MESH
        )
        return 0

    lax.fori_loop(1, n_space, greet_space, 0)
    lax.fori_loop(1, n_wave, greet_wave, 0)

    def remote(src, dst, ssem, rsem, s, w):
        return pltpu.make_async_remote_copy(
            src_ref=src,
            dst_ref=dst,
            send_sem=ssem,
            recv_sem=rsem,
            device_id=(s, w),
            device_id_type=MESH,
        )

    for copy in loads[:2]:
        copy.wait()

    for t in range(tiles):
        lanes = slice(t * TILE, (t + 1) * TILE)
        posw[tiles + t] = jnp.concatenate(
            [pos_ref[:, lanes], jnp.zeros((5, TILE), F32)], axis=0
        )

    waves = wave_ref.shape[1]
    n_all = wave_ref[...].astype(F32)
    padded = jnp.concatenate([n_all, jnp.zeros((5, waves), F32)], axis=0)
    padded = jnp.concatenate([padded] * 3, axis=0)
    nf[...] = padded.astype(BF16)
    for n in range(waves // TILE):
        at = slice(n * TILE, (n + 1) * TILE)
        nt[at, :] = jnp.transpose(padded[:, at]).astype(BF16)
    sides = jnp.where(
        lax.broadcasted_iota(jnp.int32, (8, TILE), 0) == 0, F32(1.0 / n_space), F32(1.0 / SIDE_CROSS)
    )

    def trig(angle):
        r = angle - nearest(angle)
        r2 = r * r
        half_sine = polynomial(ODD, r2) * r
        cosine = 1.0 - half_sine * half_sine
        sine = half_sine * polynomial(EVEN, r2)
        halves = []
        for value in (cosine, sine):
            high = value.astype(BF16)
            halves.append((high, (value - high.astype(F32)).astype(BF16)))
        return halves

    def tile_at(d):
        return lax.rem(wv + d, n_wave)

    def distance(j):
        if isinstance(j, int):
            return (j + 1) // 2 if j % 2 == 1 else (n_wave - j // 2) % n_wave
        half = lax.div(j + 1, 2)
        return jnp.where(lax.rem(j, 2) == 1, half, lax.rem(n_wave - half, n_wave))

    def make_phases(t):
        box = posw[tiles + tile_at(distance(t))] * sides
        first = box.astype(BF16).astype(F32)
        second = (box - first).astype(BF16).astype(F32)
        pieces = jnp.concatenate([first, second, box - first - second], axis=0)
        pf[:, pl.ds(pl.multiple_of(t * TILE, TILE), TILE)] = pieces.astype(BF16)
        turns[...] = jnp.dot(
            jnp.transpose(pieces).astype(BF16), nf[...], preferred_element_type=F32
        )
        for j in range(TILE // 16):
            rows = pl.ds(pl.multiple_of(t * TILE + j * 16, 16), 16)
            for at, (high, low) in zip((0, waves), trig(turns[j * 16 : (j + 1) * 16])):
                ph_hi[rows, at : at + waves] = high
                ph_lo[rows, at : at + waves] = low

    def make_transposed(n, _):
        block = nt[pl.ds(pl.multiple_of(n * TILE, TILE), TILE), :]
        turns_t[...] = jnp.dot(block, pf[...], preferred_element_type=F32)
        for j in range(TILE // 16):
            for pair in range(tiles // 2):
                lanes = slice(pair * 2 * TILE, (pair + 1) * 2 * TILE)
                parts = trig(turns_t[j * 16 : (j + 1) * 16, lanes])
                for at, (high, low) in zip((0, waves), parts):
                    rows = pl.ds(pl.multiple_of(at + n * TILE + j * 16, 16), 16)
                    pt_hi[pair, rows, :] = high
                    pt_lo[pair, rows, :] = low
        return 0

    step = 256

    def fold(t):
        lhs = split_rows(u[0][tiles + tile_at(distance(t))])
        rows = pl.ds(pl.multiple_of(t * TILE, TILE), TILE)
        for n in range(2 * waves // step):
            cols = slice(n * step, (n + 1) * step)
            c = jnp.dot(lhs, ph_hi[rows, cols], preferred_element_type=F32)
            c = (c[0:24] + c[24:48]) + jnp.dot(
                lhs[0:24], ph_lo[rows, cols], preferred_element_type=F32
            )
            cacc[:, cols] += c

    def fold_and_make(t, _):
        fold(t - 1)
        make_phases(t)
        return 0

    cacc[...] = jnp.zeros_like(cacc)
    make_phases(0)
    for copy in loads[2:]:
        copy.wait()
    lax.fori_loop(1, tiles, fold_and_make, 0)
    n_rows = [jnp.broadcast_to(wave_ref[c : c + 1].astype(F32), (8, waves)) for c in range(3)]
    ka = n_rows[0] * F32(2.0 * math.pi / n_space)
    kb = n_rows[1] * F32(2.0 * math.pi / SIDE_CROSS)
    kc = n_rows[2] * F32(2.0 * math.pi / SIDE_CROSS)
    plane = ka * ka + kb * kb
    square = plane + kc * kc
    scaled = square / SPLIT_SQUARE
    weight = FAR_AMP * (1.0 + scaled) * jnp.exp(-scaled) / (KW * (square + SCREEN))
    root = jnp.sqrt(weight)
    rho = jnp.sqrt(plane)
    length = jnp.sqrt(square)
    ev[0] = -root * kb / rho
    ev[1] = root * ka / rho
    ev[2] = -root * ka * kc / (rho * length)
    ev[3] = -root * kb * kc / (rho * length)
    ev[4] = root * rho / length
    fold(tiles - 1)

    def halo(k):
        own = u[k].at[pl.ds(tiles, tiles)]
        return (
            remote(own, u[k].at[pl.ds(0, tiles)], halo_s.at[k, 0], halo_r.at[k, 0], up, wv),
            remote(own, u[k].at[pl.ds(2 * tiles, tiles)], halo_s.at[k, 1], halo_r.at[k, 1], down, wv),
        )

    own_pos = posw.at[pl.ds(tiles, tiles)]
    pos_copies = (
        remote(own_pos, posw.at[pl.ds(0, tiles)], pos_s.at[0], pos_r.at[0], up, wv),
        remote(own_pos, posw.at[pl.ds(2 * tiles, tiles)], pos_s.at[1], pos_r.at[1], down, wv),
    )

    def pair_of(i):
        j = wv * (32 // n_wave) + i
        total = jnp.int32(0)
        tile = jnp.int32(0)
        base = jnp.int32(0)
        for t in range(tiles):
            total = total + counts_ref[t]
            past = total <= j
            tile = tile + past.astype(jnp.int32)
            base = jnp.where(past, total, base)
        tile = jnp.minimum(tile, tiles - 1)
        slot = jnp.clip(j - base, 0, lists_ref.shape[1] - 1)
        return tile, jnp.clip(lists_ref[tile, slot], 0, 3 * tiles - 1)

    pairs = 32 // n_wave

    def build_pair(i, _):
        tile, source = pair_of(i)
        target_rows = posw[tiles + tile]
        source_cols = jnp.transpose(posw[source])
        offs = []
        for c, side in enumerate((float(n_space), SIDE_CROSS, SIDE_CROSS)):
            off = target_rows[c : c + 1] - source_cols[:, c : c + 1]
            offs.append(off - F32(side) * jnp.floor(off * F32(1.0 / side) + 0.5))
        square = offs[0] * offs[0] + offs[1] * offs[1] + offs[2] * offs[2]
        diagonal = lax.broadcasted_iota(jnp.int32, (TILE, TILE), 0) == lax.broadcasted_iota(
            jnp.int32, (TILE, TILE), 1
        )
        own = jnp.where(source == tiles + tile, F32(0.0), F32(1.0))
        keep = jnp.where(diagonal, own, F32(1.0))
        envelope = NEAR_AMP * jnp.exp(-square / NEAR_SQUARE) * keep
        scaled_env = envelope / NEAR_SQUARE
        for a in range(3):
            left = offs[a] * scaled_env
            for b in range(a, 3):
                block = left * offs[b]
                if a == b:
                    block = block + envelope
                high = block.astype(BF16)
                low = (block - high.astype(F32)).astype(BF16)
                for p, q in sorted({(a, b), (b, a)}):
                    at = (i, slice(p * TILE, (p + 1) * TILE), slice(q * TILE, (q + 1) * TILE))
                    bm_hi[at] = high
                    bm_lo[at] = low
        return 0

    def near_apply(k):
        near[...] = jnp.zeros_like(near)

        def one_pair(i, _):
            tile, source = pair_of(i)
            f = u[k][source]
            lhs = split_rows(jnp.concatenate([f[0:8], f[8:16], f[16:24]], axis=1))
            res = jnp.dot(lhs, bm_hi[i], preferred_element_type=F32) + jnp.dot(
                lhs, bm_lo[i], preferred_element_type=F32
            )
            res = res[0:8] + res[8:16]
            res = jnp.concatenate([res[:, c * TILE : (c + 1) * TILE] for c in range(3)], axis=0)
            for t in range(tiles):
                near[t] += jnp.where(tile == t, res, 0.0)
            return 0

        lax.fori_loop(0, pairs, one_pair, 0)

    my_y, my_x, my_c = lax.div(me, 8), lax.rem(lax.div(me, 2), 4), lax.rem(me, 2)
    far = {0: 0, 1: 1, 2: 2, 3: 1}
    steps = [(dy, dx, dc) for dy in range(4) for dx in range(4) for dc in range(2)]
    steps = sorted(steps, key=lambda d: -(10 * (far[d[0]] + far[d[1]]) + d[2]))[:-1]
    n_chips = n_space // 2
    my_chip = lax.div(me, 2)
    chip_steps = [(dy, dx) for dy in range(4) for dx in range(4)]
    chip_steps = sorted(chip_steps, key=lambda d: -(far[d[0]] + far[d[1]]))

    def chip_at(dy, dx):
        return lax.rem(my_y + dy, 4) * 4 + lax.rem(my_x + dx, 4)

    ring_order = [4, 3, 5, 2, 6, 1, 7]

    def send_space(src_of, dst, ssem, rsem):
        for dy, dx, dc in steps:
            peer = lax.rem(my_y + dy, 4) * 8 + lax.rem(my_x + dx, 4) * 2 + lax.rem(my_c + dc, 2)
            remote(src_of(peer), dst, ssem, rsem, peer, wv).start()

    def all_but_one(ref, count, ssem, rsem):
        some = ref.at[pl.ds(0, count)]
        return remote(some, some, ssem, rsem, up, wv)

    sent = []

    for k in range(DEGREE):
        groups = ((0, 1), (2, 3), (4, 5), (6,), (7,)) if k > 0 else ()
        for group in groups:
            for j in group:
                d = distance(j)
                if d > 0:
                    piece = u[k].at[tiles + tile_at(d)]
                    sem = n_wave - d
                    remote(piece, piece, wa_s.at[k - 1], wa_r.at[k - 1, sem], up, wv).wait_recv()
            x = [u[k][tiles + tile_at(distance(j))] for j in group]
            lhs = split_rows(jnp.concatenate(x, axis=1))
            rows = slice(group[0] * TILE, (group[-1] + 1) * TILE)
            for n in range(2 * waves // step):
                cols = slice(n * step, (n + 1) * step)
                c = jnp.dot(lhs, ph_hi[rows, cols], preferred_element_type=F32)
                c = (c[0:24] + c[24:48]) + jnp.dot(
                    lhs[0:24], ph_lo[rows, cols], preferred_element_type=F32
                )
                if group[0] == 0:
                    cacc[:, cols] = c
                else:
                    cacc[:, cols] += c
        for n in range(waves // step):
            for half in range(2):
                c = cacc[:, half * waves + n * step : half * waves + (n + 1) * step]
                for q in range(step // TILE):
                    lanes = slice(q * TILE, (q + 1) * TILE)
                    at = slice(n * step + q * TILE, n * step + (q + 1) * TILE)
                    c0, c1, c2 = c[0:8, lanes], c[8:16, lanes], c[16:24, lanes]
                    d0 = ev[0, :, at] * c0 + ev[1, :, at] * c1
                    d1 = ev[2, :, at] * c0 + ev[3, :, at] * c1 + ev[4, :, at] * c2
                    chip = half * (waves // TILE) + n * (step // TILE) + q
                    for tangent, d in ((0, d0), (1, d1)):
                        sbuf[k, tangent * (2 * waves // TILE) + chip] = d
        if k == 0:
            pl.semaphore_wait(barrier, n_space - 1 + n_wave - 1)
        for dy, dx in chip_steps:
            peer = chip_at(dy, dx)

            def send(peer=peer):
                remote(
                    sbuf.at[k, peer], rs.at[k, me], rs_s.at[k], rs_r.at[k], 2 * peer + 1, wv
                ).start()

            if (dy, dx) == (0, 0):
                pl.when(my_c == 0)(send)
            else:
                send()

        for copy in (pos_copies if k == 0 else ()) + halo(k):
            copy.start()
        if k == 0:
            lax.fori_loop(0, waves // TILE, make_transposed, 0)

        @pl.when(my_c == 1)
        def _():
            all_but_one(rs.at[k], n_space - 1, rs_s.at[k], rs_r.at[k]).wait_recv()
            rs[k, me] = sbuf[k, my_chip]
            sums = [rs[k, s] + rs[k, s + 1] for s in range(0, n_space, 2)]
            while len(sums) > 1:
                sums = [sums[s] + sums[s + 1] for s in range(0, len(sums), 2)]
            agb[k, my_chip] = sums[0]
            for dy, dx in chip_steps:
                for c in (0, 1):
                    if (dy, dx, c) != (0, 0, 1):
                        own = agb.at[k, my_chip]
                        remote(
                            own, own, ag_s.at[k], ag_r.at[k], 2 * chip_at(dy, dx) + c, wv
                        ).start()

        if k > 0:
            total = jnp.zeros((8, TILE), F32)
            for t in range(tiles):
                v = u[k][tiles + t]
                v = v * v
                total = total + (v[0:8] + v[8:16] + v[16:24])
            lane_sum = jnp.sum(total, axis=1, keepdims=True)
            pick = lax.broadcasted_iota(jnp.int32, (8, TILE), 0) == lax.broadcasted_iota(
                jnp.int32, (8, TILE), 1
            )
            row = jnp.sum(jnp.where(pick, lane_sum, 0.0), axis=0, keepdims=True)
            nsrc[k - 1] = row
            nrecv[k - 1, me] = row
            send_space(
                lambda peer: nsrc.at[k - 1],
                nrecv.at[k - 1, me],
                norm_s.at[k - 1],
                norm_r.at[k - 1],
            )
            sent.append((nrecv.at[k - 1], n_space - 1, norm_s.at[k - 1], norm_r.at[k - 1]))

        if k == 0:
            for copy in pos_copies:
                copy.wait_recv()
            lax.fori_loop(0, pairs, build_pair, 0)
        for copy in halo(k):
            copy.wait_recv()
        near_apply(k)

        @pl.when(my_c == 0)
        def _():
            all_but_one(agb.at[k], n_chips, ag_s.at[k], ag_r.at[k]).wait_recv()

        @pl.when(my_c == 1)
        def _():
            all_but_one(agb.at[k], n_chips - 1, ag_s.at[k], ag_r.at[k]).wait_recv()


        rows = [[], [], []]
        for half in range(2):
            for n in range(waves // TILE):
                at = slice(n * TILE, (n + 1) * TILE)
                chip = half * (waves // TILE) + n
                d = []
                for tangent in range(2):
                    d.append(agb[k, tangent * (2 * waves // TILE) + chip])
                rows[0].append(ev[0, :, at] * d[0] + ev[2, :, at] * d[1])
                rows[1].append(ev[1, :, at] * d[0] + ev[3, :, at] * d[1])
                rows[2].append(ev[4, :, at] * d[1])
        lhs = split_rows(
            jnp.concatenate([jnp.concatenate(r, axis=1) for r in rows], axis=0)
        )
        back[...] = lhs

        def back_pair(i, _):
            pair = tiles // 2 - 1 - i
            v = jnp.dot(back[...], pt_hi[pair], preferred_element_type=F32)
            v = (v[0:24] + v[24:48]) + jnp.dot(
                back[0:24, :], pt_lo[pair], preferred_element_type=F32
            )

            def part(d, q):
                t = tile_at(d)
                vbuf[k, t] = v[:, q * TILE : (q + 1) * TILE] + near[t]
                return t

            def send(t):
                remote(vbuf.at[k, t], wr.at[k, wv], wr_s.at[k], wr_r.at[k], me, t).start()

            send(part(distance(2 * pair + 1), 1))
            t = part(distance(2 * pair), 0)

            @pl.when(pair > 0)
            def _():
                send(t)

            return 0

        lax.fori_loop(0, n_wave // 2, back_pair, 0)
        wr[k, wv] = vbuf[k, wv] + u[k][tiles + wv]
        sent.append((wr.at[k], n_wave - 1, wr_s.at[k], wr_r.at[k]))
        if k == DEGREE - 1:
            for j in range(2):
                all_but_one(nrecv.at[j], n_space - 1, norm_s.at[j], norm_r.at[j]).wait_recv()
            sums = []
            for j in range(2):
                total = nrecv[j, 0]
                for s in range(1, n_space):
                    total = total + nrecv[j, s]
                sums.append(total)
            ratio = jnp.max(sums[1] / (sums[0] + EPSILON), axis=1, keepdims=True)
            high = SAFETY * jnp.sqrt(jnp.broadcast_to(ratio, (8, TILE)))
            low = high / SPREAD
            nodes = DEGREE + 1
            angles = [(j + 0.5) * math.pi / nodes for j in range(nodes)]
            samples = [
                jnp.sqrt(0.5 * (high - low) * F32(math.cos(a)) + 0.5 * (high + low)) for a in angles
            ]
            coeffs = []
            for order in range(nodes):
                c = samples[0] * F32(math.cos(order * angles[0]))
                for j in range(1, nodes):
                    c = c + samples[j] * F32(math.cos(order * angles[j]))
                coeffs.append(c * F32((1.0 if order == 0 else 2.0) / nodes))
            bound_sum = high + low
            scale = 1.0 / (high - low)
        all_but_one(wr.at[k], n_wave - 1, wr_s.at[k], wr_r.at[k]).wait_recv()
        image = wr[k, 0]
        for w in range(1, n_wave):
            image = image + wr[k, w]

        if k < DEGREE - 1:
            own = u[k + 1].at[tiles + wv]
            u[k + 1][tiles + wv] = image
            whole = u[k + 1].at[pl.ds(tiles, tiles)]
        else:
            pieces = []
            for c in range(3):
                at = slice(c * 8, (c + 1) * 8)
                f = u[0][tiles + wv, at]
                u1 = u[1][tiles + wv, at]
                u2 = u[2][tiles + wv, at]
                u3 = image[at]
                t1 = (2.0 * u1 - bound_sum * f) * scale
                mt1 = (2.0 * u2 - bound_sum * u1) * scale
                mmt1 = (2.0 * u3 - bound_sum * u2) * scale
                t2 = 2.0 * (2.0 * mt1 - bound_sum * t1) * scale - f
                mt2 = 2.0 * (2.0 * mmt1 - bound_sum * mt1) * scale - u1
                t3 = 2.0 * (2.0 * mt2 - bound_sum * t2) * scale - t1
                pieces.append(coeffs[0] * f + coeffs[1] * t1 + coeffs[2] * t2 + coeffs[3] * t3)
            own = outb.at[wv]
            outb[wv] = jnp.concatenate(pieces, axis=0)
            whole = outb

        for d in ring_order:
            remote(own, own, wa_s.at[k], wa_r.at[k, d], me, tile_at(d)).start()
        sent.append((whole, n_wave - 1, wa_s.at[k], wa_r.at[k, 0]))

    def put(t):
        out_ref[:, pl.ds(pl.multiple_of(t * TILE, TILE), TILE)] = outb[t]

    put(wv)
    for d in (1, 7, 2, 6, 3, 5, 4):
        piece = outb.at[tile_at(d)]
        remote(piece, piece, wa_s.at[2], wa_r.at[2, n_wave - d], up, wv).wait_recv()
        put(tile_at(d))
    for k in range(DEGREE):

        @pl.when(my_c == 0)
        def _():
            all_but_one(sbuf.at[k], n_chips, rs_s.at[k], rs_r.at[k]).wait_send()

        @pl.when(my_c == 1)
        def _():
            all_but_one(sbuf.at[k], n_chips - 1, rs_s.at[k], rs_r.at[k]).wait_send()
            all_but_one(rs.at[k], n_space - 1, ag_s.at[k], ag_r.at[k]).wait_send()

    for ref, count, ssem, rsem in sent:
        all_but_one(ref, count, ssem, rsem).wait_send()
    for copy in pos_copies:
        copy.wait_send()
    for k in range(DEGREE):
        for copy in halo(k):
            copy.wait_send()


def body(n_space, n_wave, noise, positions, wave_index, tile_lists, tile_counts):
    tiles = positions.shape[1] // TILE
    count = positions.shape[1]
    waves = wave_index.shape[1]
    vectors = noise.shape[0]
    rows = vectors * 3
    arranged = jnp.transpose(noise, (1, 0, 2)).reshape(rows, count)
    pairs = 32 // n_wave
    vmem = pl.BlockSpec(memory_space=pltpu.VMEM)
    dma = pltpu.SemaphoreType.DMA

    hbm = pl.BlockSpec(memory_space=pl.ANY)
    out = pl.pallas_call(
        functools.partial(kernel, n_space, n_wave),
        out_shape=pltpu.VMEM((rows, count), F32),
        in_specs=[hbm] * 5,
        out_specs=vmem,
        scratch_shapes=[
            pltpu.VMEM((3, count), F32),
            pltpu.VMEM((3, waves), jnp.int32),
            pltpu.SMEM(tile_lists.shape, jnp.int32),
            pltpu.SMEM(tile_counts.shape, jnp.int32),
            pltpu.VMEM((rows, 2 * waves), F32),
            pltpu.VMEM((2 * rows, 2 * waves), BF16),
            pltpu.VMEM((count, 2 * waves), BF16),
            pltpu.VMEM((count, 2 * waves), BF16),
            pltpu.VMEM((tiles // 2, 2 * waves, 2 * TILE), BF16),
            pltpu.VMEM((tiles // 2, 2 * waves, 2 * TILE), BF16),
            pltpu.VMEM((3 * tiles, 8, TILE), F32),
            pltpu.VMEM((5, 8, waves), F32),
            pltpu.VMEM((24, waves), BF16),
            pltpu.VMEM((waves, 24), BF16),
            pltpu.VMEM((24, count), BF16),
            pltpu.VMEM((TILE, waves), F32),
            pltpu.VMEM((TILE, count), F32),
            pltpu.VMEM((pairs, 3 * TILE, 3 * TILE), BF16),
            pltpu.VMEM((pairs, 3 * TILE, 3 * TILE), BF16),
            pltpu.VMEM((3 * tiles, rows, TILE), F32),
            pltpu.VMEM((3 * tiles, rows, TILE), F32),
            pltpu.VMEM((3 * tiles, rows, TILE), F32),
            pltpu.VMEM((tiles, rows, TILE), F32),
            pltpu.VMEM((DEGREE, n_space // 2, 8, TILE), F32),
            pltpu.VMEM((DEGREE, n_space, 8, TILE), F32),
            pltpu.VMEM((DEGREE, n_space // 2, 8, TILE), F32),
            pltpu.VMEM((DEGREE, tiles, rows, TILE), F32),
            pltpu.VMEM((DEGREE, tiles, rows, TILE), F32),
            pltpu.VMEM((2, 1, TILE), F32),
            pltpu.VMEM((2, n_space, 1, TILE), F32),
            pltpu.VMEM((tiles, rows, TILE), F32),
            dma((DEGREE,)),
            dma((DEGREE,)),
            dma((DEGREE,)),
            dma((DEGREE,)),
            dma((DEGREE,)),
            dma((DEGREE,)),
            dma((DEGREE,)),
            dma((DEGREE, n_wave)),
            dma((DEGREE, 2)),
            dma((DEGREE, 2)),
            dma((2,)),
            dma((2,)),
            dma((2,)),
            dma((2,)),
            dma((4 + tiles,)),
        ],
        compiler_params=pltpu.CompilerParams(
            collective_id=0, has_side_effects=True, vmem_limit_bytes=60 * 1024 * 1024
        ),
    )(arranged, positions, wave_index, tile_lists, tile_counts)
    return jnp.transpose(out.reshape(3, vectors, count), (1, 0, 2))


def solution(mesh):
    n_space, n_wave = mesh.shape["space"], mesh.shape["wave"]

    def step(*args):
        return body(n_space, n_wave, *args)

    in_specs = (
        P(None, None, "space"),
        P(None, "space"),
        P(None, "wave"),
        P("space", None),
        P("space"),
    )
    out_specs = P(None, None, "space")
    return jax.shard_map(step, mesh=mesh, in_specs=in_specs, out_specs=out_specs, check_vma=False)
```

```python
import functools
import math

import jax
import jax.numpy as jnp
from jax import lax
from jax.experimental import pallas as pl
from jax.experimental.pallas import tpu as pltpu
from jax.sharding import PartitionSpec as P

MESH = pl.DeviceIdType.MESH
F32 = jnp.float32
BF16 = jnp.bfloat16

KW = 4096
DEGREE = 3
TILE = 128
SIDE_CROSS = 8.0
NEAR_SQUARE = 0.36
NEAR_AMP = 0.15
FAR_AMP = 8.0
SPLIT_SQUARE = 64.0
SCREEN = 4.0
SAFETY = 1.25
SPREAD = 100.0
EPSILON = 1e-06

ODD = (4.442882834148948, -7.308241154482914, 3.6062889571583123, -0.8457635896353835, 0.10920574060672703)
EVEN = (1.4142134965574307, -6.978850987759868, 5.7394611627073875, -1.8835629390376682, 0.31069809581455876)


def split_rows(x):
    high = x.astype(BF16).astype(F32)
    return jnp.concatenate([high, x - high], axis=0).astype(BF16)


def nearest(x):
    return lax.round(x, lax.RoundingMethod.TO_NEAREST_EVEN)


def polynomial(coeffs, x):
    p = F32(coeffs[-1])
    for c in coeffs[-2::-1]:
        p = p * x + F32(c)
    return p


def kernel(
    n_space,
    n_wave,
    noise_hbm,
    pos_hbm,
    wave_hbm,
    lists_hbm,
    counts_hbm,
    out_ref,
    pos_ref,
    wave_ref,
    lists_ref,
    counts_ref,
    cacc,
    back,
    ph_hi,
    ph_lo,
    pt_hi,
    pt_lo,
    posw,
    ev,
    nf,
    nt,
    pf,
    turns,
    turns_t,
    bm_hi,
    bm_lo,
    u0,
    u1_,
    u2_,
    near,
    sbuf,
    rs,
    agb,
    vbuf,
    wr,
    nsrc,
    nrecv,
    outb,
    rs_s,
    rs_r,
    ag_s,
    ag_r,
    wr_s,
    wr_r,
    wa_s,
    wa_r,
    halo_s,
    halo_r,
    pos_s,
    pos_r,
    norm_s,
    norm_r,
    in_s,
):
    me = lax.axis_index("space")
    wv = lax.axis_index("wave")
    up = lax.rem(me + 1, n_space)
    down = lax.rem(me + n_space - 1, n_space)
    tiles = n_wave
    u = (u0, u1_, u2_)

    loads = [
        pltpu.make_async_copy(pos_hbm, pos_ref, in_s.at[0]),
        pltpu.make_async_copy(wave_hbm, wave_ref, in_s.at[1]),
    ]
    for t in range(tiles):
        loads.append(
            pltpu.make_async_copy(
                noise_hbm.at[:, pl.ds(t * TILE, TILE)], u[0].at[tiles + t], in_s.at[4 + t]
            )
        )
    loads.append(pltpu.make_async_copy(lists_hbm, lists_ref, in_s.at[2]))
    loads.append(pltpu.make_async_copy(counts_hbm, counts_ref, in_s.at[3]))
    for copy in loads:
        copy.start()

    barrier = pltpu.get_barrier_semaphore()

    ring = (0, 1, 2, 1)
    greeted = sorted(range(1, n_space), key=lambda d: -(ring[d // 8] + ring[d // 2 % 4]))
    peers = [(lax.rem(me + d, n_space), wv) for d in greeted]
    peers = [(me, lax.rem(wv + d, n_wave)) for d in (4, 3, 5, 2, 6, 1, 7)] + peers
    for peer in peers:
        pl.semaphore_signal(barrier, inc=1, device_id=peer, device_id_type=MESH)

    def remote(src, dst, ssem, rsem, s, w):
        return pltpu.make_async_remote_copy(
            src_ref=src,
            dst_ref=dst,
            send_sem=ssem,
            recv_sem=rsem,
            device_id=(s, w),
            device_id_type=MESH,
        )

    for copy in loads[:2]:
        copy.wait()

    for t in range(tiles):
        lanes = slice(t * TILE, (t + 1) * TILE)
        posw[tiles + t] = jnp.concatenate(
            [pos_ref[:, lanes], jnp.zeros((5, TILE), F32)], axis=0
        )

    waves = wave_ref.shape[1]
    n_all = wave_ref[...].astype(F32)
    padded = jnp.concatenate([n_all, jnp.zeros((5, waves), F32)], axis=0)
    padded = jnp.concatenate([padded] * 3, axis=0)
    nf[...] = padded.astype(BF16)
    for n in range(waves // TILE):
        at = slice(n * TILE, (n + 1) * TILE)
        nt[at, :] = jnp.transpose(padded[:, at]).astype(BF16)
    sides = jnp.where(
        lax.broadcasted_iota(jnp.int32, (8, TILE), 0) == 0, F32(1.0 / n_space), F32(1.0 / SIDE_CROSS)
    )

    def trig(angle):
        r = angle - nearest(angle)
        r2 = r * r
        half_sine = polynomial(ODD, r2) * r
        cosine = 1.0 - half_sine * half_sine
        sine = half_sine * polynomial(EVEN, r2)
        halves = []
        for value in (cosine, sine):
            high = value.astype(BF16)
            halves.append((high, (value - high.astype(F32)).astype(BF16)))
        return halves

    def tile_at(d):
        return lax.rem(wv + d, n_wave)

    def distance(j):
        if isinstance(j, int):
            return (j + 1) // 2 if j % 2 == 1 else (n_wave - j // 2) % n_wave
        half = lax.div(j + 1, 2)
        return jnp.where(lax.rem(j, 2) == 1, half, lax.rem(n_wave - half, n_wave))

    def make_phases(t):
        box = posw[tiles + tile_at(distance(t))] * sides
        first = box.astype(BF16).astype(F32)
        second = (box - first).astype(BF16).astype(F32)
        pieces = jnp.concatenate([first, second, box - first - second], axis=0)
        pf[:, pl.ds(pl.multiple_of(t * TILE, TILE), TILE)] = pieces.astype(BF16)
        turns[...] = jnp.dot(
            jnp.transpose(pieces).astype(BF16), nf[...], preferred_element_type=F32
        )
        for j in range(TILE // 16):
            rows = pl.ds(pl.multiple_of(t * TILE + j * 16, 16), 16)
            for at, (high, low) in zip((0, waves), trig(turns[j * 16 : (j + 1) * 16])):
                ph_hi[rows, at : at + waves] = high
                ph_lo[rows, at : at + waves] = low

    def make_transposed(n, _):
        block = nt[pl.ds(pl.multiple_of(n * TILE, TILE), TILE), :]
        turns_t[...] = jnp.dot(block, pf[...], preferred_element_type=F32)
        for j in range(TILE // 16):
            for pair in range(tiles // 2):
                lanes = slice(pair * 2 * TILE, (pair + 1) * 2 * TILE)
                parts = trig(turns_t[j * 16 : (j + 1) * 16, lanes])
                for at, (high, low) in zip((0, waves), parts):
                    rows = pl.ds(pl.multiple_of(at + n * TILE + j * 16, 16), 16)
                    pt_hi[pair, rows, :] = high
                    pt_lo[pair, rows, :] = low
        return 0

    step = 256

    def fold(t):
        lhs = split_rows(u[0][tiles + tile_at(distance(t))])
        rows = pl.ds(pl.multiple_of(t * TILE, TILE), TILE)
        for n in range(2 * waves // step):
            cols = slice(n * step, (n + 1) * step)
            c = jnp.dot(lhs, ph_hi[rows, cols], preferred_element_type=F32)
            c = (c[0:24] + c[24:48]) + jnp.dot(
                lhs[0:24], ph_lo[rows, cols], preferred_element_type=F32
            )
            cacc[:, cols] += c

    def fold_and_make(t, _):
        fold(t - 1)
        make_phases(t)
        return 0

    cacc[...] = jnp.zeros_like(cacc)
    make_phases(0)
    for copy in loads[2:]:
        copy.wait()
    lax.fori_loop(1, tiles, fold_and_make, 0)
    n_rows = [jnp.broadcast_to(wave_ref[c : c + 1].astype(F32), (8, waves)) for c in range(3)]
    ka = n_rows[0] * F32(2.0 * math.pi / n_space)
    kb = n_rows[1] * F32(2.0 * math.pi / SIDE_CROSS)
    kc = n_rows[2] * F32(2.0 * math.pi / SIDE_CROSS)
    plane = ka * ka + kb * kb
    square = plane + kc * kc
    scaled = square / SPLIT_SQUARE
    weight = FAR_AMP * (1.0 + scaled) * jnp.exp(-scaled) / (KW * (square + SCREEN))
    root = jnp.sqrt(weight)
    rho = jnp.sqrt(plane)
    length = jnp.sqrt(square)
    ev[0] = -root * kb / rho
    ev[1] = root * ka / rho
    ev[2] = -root * ka * kc / (rho * length)
    ev[3] = -root * kb * kc / (rho * length)
    ev[4] = root * rho / length
    fold(tiles - 1)

    def halo(k):
        own = u[k].at[pl.ds(tiles, tiles)]
        return (
            remote(own, u[k].at[pl.ds(0, tiles)], halo_s.at[k, 0], halo_r.at[k, 0], up, wv),
            remote(own, u[k].at[pl.ds(2 * tiles, tiles)], halo_s.at[k, 1], halo_r.at[k, 1], down, wv),
        )

    own_pos = posw.at[pl.ds(tiles, tiles)]
    pos_copies = (
        remote(own_pos, posw.at[pl.ds(0, tiles)], pos_s.at[0], pos_r.at[0], up, wv),
        remote(own_pos, posw.at[pl.ds(2 * tiles, tiles)], pos_s.at[1], pos_r.at[1], down, wv),
    )

    def pair_of(i):
        j = wv * (32 // n_wave) + i
        total = jnp.int32(0)
        tile = jnp.int32(0)
        base = jnp.int32(0)
        for t in range(tiles):
            total = total + counts_ref[t]
            past = total <= j
            tile = tile + past.astype(jnp.int32)
            base = jnp.where(past, total, base)
        tile = jnp.minimum(tile, tiles - 1)
        slot = jnp.clip(j - base, 0, lists_ref.shape[1] - 1)
        return tile, jnp.clip(lists_ref[tile, slot], 0, 3 * tiles - 1)

    pairs = 32 // n_wave

    def build_pair(i, _):
        tile, source = pair_of(i)
        target_rows = posw[tiles + tile]
        source_cols = jnp.transpose(posw[source])
        offs = []
        for c, side in enumerate((float(n_space), SIDE_CROSS, SIDE_CROSS)):
            off = target_rows[c : c + 1] - source_cols[:, c : c + 1]
            offs.append(off - F32(side) * jnp.floor(off * F32(1.0 / side) + 0.5))
        square = offs[0] * offs[0] + offs[1] * offs[1] + offs[2] * offs[2]
        diagonal = lax.broadcasted_iota(jnp.int32, (TILE, TILE), 0) == lax.broadcasted_iota(
            jnp.int32, (TILE, TILE), 1
        )
        own = jnp.where(source == tiles + tile, F32(0.0), F32(1.0))
        keep = jnp.where(diagonal, own, F32(1.0))
        envelope = NEAR_AMP * jnp.exp(-square / NEAR_SQUARE) * keep
        scaled_env = envelope / NEAR_SQUARE
        for a in range(3):
            left = offs[a] * scaled_env
            for b in range(a, 3):
                block = left * offs[b]
                if a == b:
                    block = block + envelope
                high = block.astype(BF16)
                low = (block - high.astype(F32)).astype(BF16)
                for p, q in sorted({(a, b), (b, a)}):
                    at = (i, slice(p * TILE, (p + 1) * TILE), slice(q * TILE, (q + 1) * TILE))
                    bm_hi[at] = high
                    bm_lo[at] = low
        return 0

    def near_apply(k):
        near[...] = jnp.zeros_like(near)

        def one_pair(i, _):
            tile, source = pair_of(i)
            f = u[k][source]
            lhs = split_rows(jnp.concatenate([f[0:8], f[8:16], f[16:24]], axis=1))
            res = jnp.dot(lhs, bm_hi[i], preferred_element_type=F32) + jnp.dot(
                lhs, bm_lo[i], preferred_element_type=F32
            )
            res = res[0:8] + res[8:16]
            res = jnp.concatenate([res[:, c * TILE : (c + 1) * TILE] for c in range(3)], axis=0)
            for t in range(tiles):
                near[t] += jnp.where(tile == t, res, 0.0)
            return 0

        lax.fori_loop(0, pairs, one_pair, 0)

    my_y, my_x, my_c = lax.div(me, 8), lax.rem(lax.div(me, 2), 4), lax.rem(me, 2)
    far = {0: 0, 1: 1, 2: 2, 3: 1}
    steps = [(dy, dx, dc) for dy in range(4) for dx in range(4) for dc in range(2)]
    steps = sorted(steps, key=lambda d: -(10 * (far[d[0]] + far[d[1]]) + d[2]))[:-1]
    n_chips = n_space // 2
    my_chip = lax.div(me, 2)
    chip_steps = [(dy, dx) for dy in range(4) for dx in range(4)]
    chip_steps = sorted(chip_steps, key=lambda d: -(far[d[0]] + far[d[1]]))

    def chip_at(dy, dx):
        return lax.rem(my_y + dy, 4) * 4 + lax.rem(my_x + dx, 4)

    ring_order = [4, 3, 5, 2, 6, 1, 7]

    def send_space(src_of, dst, ssem, rsem):
        for dy, dx, dc in steps:
            peer = lax.rem(my_y + dy, 4) * 8 + lax.rem(my_x + dx, 4) * 2 + lax.rem(my_c + dc, 2)
            remote(src_of(peer), dst, ssem, rsem, peer, wv).start()

    def all_but_one(ref, count, ssem, rsem):
        some = ref.at[pl.ds(0, count)]
        return remote(some, some, ssem, rsem, up, wv)

    sent = []

    for k in range(DEGREE):
        groups = ((0, 1), (2, 3), (4, 5), (6,), (7,)) if k > 0 else ()
        for group in groups:
            for j in group:
                d = distance(j)
                if d > 0:
                    piece = u[k].at[tiles + tile_at(d)]
                    sem = n_wave - d
                    remote(piece, piece, wa_s.at[k - 1], wa_r.at[k - 1, sem], up, wv).wait_recv()
            x = [u[k][tiles + tile_at(distance(j))] for j in group]
            lhs = split_rows(jnp.concatenate(x, axis=1))
            rows = slice(group[0] * TILE, (group[-1] + 1) * TILE)
            for n in range(2 * waves // step):
                cols = slice(n * step, (n + 1) * step)
                c = jnp.dot(lhs, ph_hi[rows, cols], preferred_element_type=F32)
                c = (c[0:24] + c[24:48]) + jnp.dot(
                    lhs[0:24], ph_lo[rows, cols], preferred_element_type=F32
                )
                if group[0] == 0:
                    cacc[:, cols] = c
                else:
                    cacc[:, cols] += c
        for n in range(waves // step):
            for half in range(2):
                c = cacc[:, half * waves + n * step : half * waves + (n + 1) * step]
                for q in range(step // TILE):
                    lanes = slice(q * TILE, (q + 1) * TILE)
                    at = slice(n * step + q * TILE, n * step + (q + 1) * TILE)
                    c0, c1, c2 = c[0:8, lanes], c[8:16, lanes], c[16:24, lanes]
                    d0 = ev[0, :, at] * c0 + ev[1, :, at] * c1
                    d1 = ev[2, :, at] * c0 + ev[3, :, at] * c1 + ev[4, :, at] * c2
                    chip = half * (waves // TILE) + n * (step // TILE) + q
                    for tangent, d in ((0, d0), (1, d1)):
                        sbuf[k, tangent * (2 * waves // TILE) + chip] = d
        if k == 0:
            pl.semaphore_wait(barrier, n_space - 1 + n_wave - 1)
        for dy, dx in chip_steps:
            peer = chip_at(dy, dx)

            def send(peer=peer):
                remote(
                    sbuf.at[k, peer], rs.at[k, me], rs_s.at[k], rs_r.at[k], 2 * peer + 1, wv
                ).start()

            if (dy, dx) == (0, 0):
                pl.when(my_c == 0)(send)
            else:
                send()

        for copy in (pos_copies if k == 0 else ()) + halo(k):
            copy.start()
        if k == 0:
            lax.fori_loop(0, waves // TILE, make_transposed, 0)

        @pl.when(my_c == 1)
        def _():
            all_but_one(rs.at[k], n_space - 1, rs_s.at[k], rs_r.at[k]).wait_recv()
            rs[k, me] = sbuf[k, my_chip]
            sums = [rs[k, s] + rs[k, s + 1] for s in range(0, n_space, 2)]
            while len(sums) > 1:
                sums = [sums[s] + sums[s + 1] for s in range(0, len(sums), 2)]
            agb[k, my_chip] = sums[0]
            for dy, dx in chip_steps:
                for c in (0, 1):
                    if (dy, dx, c) != (0, 0, 1):
                        own = agb.at[k, my_chip]
                        remote(
                            own, own, ag_s.at[k], ag_r.at[k], 2 * chip_at(dy, dx) + c, wv
                        ).start()

        if k > 0:
            total = jnp.zeros((8, TILE), F32)
            for t in range(tiles):
                v = u[k][tiles + t]
                v = v * v
                total = total + (v[0:8] + v[8:16] + v[16:24])
            lane_sum = jnp.sum(total, axis=1, keepdims=True)
            pick = lax.broadcasted_iota(jnp.int32, (8, TILE), 0) == lax.broadcasted_iota(
                jnp.int32, (8, TILE), 1
            )
            row = jnp.sum(jnp.where(pick, lane_sum, 0.0), axis=0, keepdims=True)
            nsrc[k - 1] = row
            nrecv[k - 1, me] = row
            send_space(
                lambda peer: nsrc.at[k - 1],
                nrecv.at[k - 1, me],
                norm_s.at[k - 1],
                norm_r.at[k - 1],
            )
            sent.append((nrecv.at[k - 1], n_space - 1, norm_s.at[k - 1], norm_r.at[k - 1]))

        if k == 0:
            for copy in pos_copies:
                copy.wait_recv()
            lax.fori_loop(0, pairs, build_pair, 0)
        for copy in halo(k):
            copy.wait_recv()
        near_apply(k)

        @pl.when(my_c == 0)
        def _():
            all_but_one(agb.at[k], n_chips, ag_s.at[k], ag_r.at[k]).wait_recv()

        @pl.when(my_c == 1)
        def _():
            all_but_one(agb.at[k], n_chips - 1, ag_s.at[k], ag_r.at[k]).wait_recv()


        rows = [[], [], []]
        for half in range(2):
            for n in range(waves // TILE):
                at = slice(n * TILE, (n + 1) * TILE)
                chip = half * (waves // TILE) + n
                d = []
                for tangent in range(2):
                    d.append(agb[k, tangent * (2 * waves // TILE) + chip])
                rows[0].append(ev[0, :, at] * d[0] + ev[2, :, at] * d[1])
                rows[1].append(ev[1, :, at] * d[0] + ev[3, :, at] * d[1])
                rows[2].append(ev[4, :, at] * d[1])
        lhs = split_rows(
            jnp.concatenate([jnp.concatenate(r, axis=1) for r in rows], axis=0)
        )
        back[...] = lhs

        def back_pair(i, _):
            pair = tiles // 2 - 1 - i
            v = jnp.dot(back[...], pt_hi[pair], preferred_element_type=F32)
            v = (v[0:24] + v[24:48]) + jnp.dot(
                back[0:24, :], pt_lo[pair], preferred_element_type=F32
            )

            def part(d, q):
                t = tile_at(d)
                vbuf[k, t] = v[:, q * TILE : (q + 1) * TILE] + near[t]
                return t

            def send(t):
                remote(vbuf.at[k, t], wr.at[k, wv], wr_s.at[k], wr_r.at[k], me, t).start()

            send(part(distance(2 * pair + 1), 1))
            t = part(distance(2 * pair), 0)

            @pl.when(pair > 0)
            def _():
                send(t)

            return 0

        lax.fori_loop(0, n_wave // 2, back_pair, 0)
        wr[k, wv] = vbuf[k, wv] + u[k][tiles + wv]
        sent.append((wr.at[k], n_wave - 1, wr_s.at[k], wr_r.at[k]))
        if k == DEGREE - 1:
            for j in range(2):
                all_but_one(nrecv.at[j], n_space - 1, norm_s.at[j], norm_r.at[j]).wait_recv()
            sums = []
            for j in range(2):
                total = nrecv[j, 0]
                for s in range(1, n_space):
                    total = total + nrecv[j, s]
                sums.append(total)
            ratio = jnp.max(sums[1] / (sums[0] + EPSILON), axis=1, keepdims=True)
            high = SAFETY * jnp.sqrt(jnp.broadcast_to(ratio, (8, TILE)))
            low = high / SPREAD
            nodes = DEGREE + 1
            angles = [(j + 0.5) * math.pi / nodes for j in range(nodes)]
            samples = [
                jnp.sqrt(0.5 * (high - low) * F32(math.cos(a)) + 0.5 * (high + low)) for a in angles
            ]
            coeffs = []
            for order in range(nodes):
                c = samples[0] * F32(math.cos(order * angles[0]))
                for j in range(1, nodes):
                    c = c + samples[j] * F32(math.cos(order * angles[j]))
                coeffs.append(c * F32((1.0 if order == 0 else 2.0) / nodes))
            bound_sum = high + low
            scale = 1.0 / (high - low)
        all_but_one(wr.at[k], n_wave - 1, wr_s.at[k], wr_r.at[k]).wait_recv()
        image = wr[k, 0]
        for w in range(1, n_wave):
            image = image + wr[k, w]

        if k < DEGREE - 1:
            own = u[k + 1].at[tiles + wv]
            u[k + 1][tiles + wv] = image
            whole = u[k + 1].at[pl.ds(tiles, tiles)]
        else:
            pieces = []
            for c in range(3):
                at = slice(c * 8, (c + 1) * 8)
                f = u[0][tiles + wv, at]
                u1 = u[1][tiles + wv, at]
                u2 = u[2][tiles + wv, at]
                u3 = image[at]
                t1 = (2.0 * u1 - bound_sum * f) * scale
                mt1 = (2.0 * u2 - bound_sum * u1) * scale
                mmt1 = (2.0 * u3 - bound_sum * u2) * scale
                t2 = 2.0 * (2.0 * mt1 - bound_sum * t1) * scale - f
                mt2 = 2.0 * (2.0 * mmt1 - bound_sum * mt1) * scale - u1
                t3 = 2.0 * (2.0 * mt2 - bound_sum * t2) * scale - t1
                pieces.append(coeffs[0] * f + coeffs[1] * t1 + coeffs[2] * t2 + coeffs[3] * t3)
            own = outb.at[wv]
            outb[wv] = jnp.concatenate(pieces, axis=0)
            whole = outb

        for d in ring_order:
            remote(own, own, wa_s.at[k], wa_r.at[k, d], me, tile_at(d)).start()
        sent.append((whole, n_wave - 1, wa_s.at[k], wa_r.at[k, 0]))

    def put(t):
        out_ref[:, pl.ds(pl.multiple_of(t * TILE, TILE), TILE)] = outb[t]

    put(wv)
    for d in (1, 7, 2, 6, 3, 5, 4):
        piece = outb.at[tile_at(d)]
        remote(piece, piece, wa_s.at[2], wa_r.at[2, n_wave - d], up, wv).wait_recv()
        put(tile_at(d))
    for k in range(DEGREE):

        @pl.when(my_c == 0)
        def _():
            all_but_one(sbuf.at[k], n_chips, rs_s.at[k], rs_r.at[k]).wait_send()

        @pl.when(my_c == 1)
        def _():
            all_but_one(sbuf.at[k], n_chips - 1, rs_s.at[k], rs_r.at[k]).wait_send()
            all_but_one(rs.at[k], n_space - 1, ag_s.at[k], ag_r.at[k]).wait_send()

    for ref, count, ssem, rsem in sent:
        all_but_one(ref, count, ssem, rsem).wait_send()
    for copy in pos_copies:
        copy.wait_send()
    for k in range(DEGREE):
        for copy in halo(k):
            copy.wait_send()


def body(n_space, n_wave, noise, positions, wave_index, tile_lists, tile_counts):
    tiles = positions.shape[1] // TILE
    count = positions.shape[1]
    waves = wave_index.shape[1]
    vectors = noise.shape[0]
    rows = vectors * 3
    arranged = jnp.transpose(noise, (1, 0, 2)).reshape(rows, count)
    pairs = 32 // n_wave
    vmem = pl.BlockSpec(memory_space=pltpu.VMEM)
    dma = pltpu.SemaphoreType.DMA

    hbm = pl.BlockSpec(memory_space=pl.ANY)
    out = pl.pallas_call(
        functools.partial(kernel, n_space, n_wave),
        out_shape=pltpu.VMEM((rows, count), F32),
        in_specs=[hbm] * 5,
        out_specs=vmem,
        scratch_shapes=[
            pltpu.VMEM((3, count), F32),
            pltpu.VMEM((3, waves), jnp.int32),
            pltpu.SMEM(tile_lists.shape, jnp.int32),
            pltpu.SMEM(tile_counts.shape, jnp.int32),
            pltpu.VMEM((rows, 2 * waves), F32),
            pltpu.VMEM((2 * rows, 2 * waves), BF16),
            pltpu.VMEM((count, 2 * waves), BF16),
            pltpu.VMEM((count, 2 * waves), BF16),
            pltpu.VMEM((tiles // 2, 2 * waves, 2 * TILE), BF16),
            pltpu.VMEM((tiles // 2, 2 * waves, 2 * TILE), BF16),
            pltpu.VMEM((3 * tiles, 8, TILE), F32),
            pltpu.VMEM((5, 8, waves), F32),
            pltpu.VMEM((24, waves), BF16),
            pltpu.VMEM((waves, 24), BF16),
            pltpu.VMEM((24, count), BF16),
            pltpu.VMEM((TILE, waves), F32),
            pltpu.VMEM((TILE, count), F32),
            pltpu.VMEM((pairs, 3 * TILE, 3 * TILE), BF16),
            pltpu.VMEM((pairs, 3 * TILE, 3 * TILE), BF16),
            pltpu.VMEM((3 * tiles, rows, TILE), F32),
            pltpu.VMEM((3 * tiles, rows, TILE), F32),
            pltpu.VMEM((3 * tiles, rows, TILE), F32),
            pltpu.VMEM((tiles, rows, TILE), F32),
            pltpu.VMEM((DEGREE, n_space // 2, 8, TILE), F32),
            pltpu.VMEM((DEGREE, n_space, 8, TILE), F32),
            pltpu.VMEM((DEGREE, n_space // 2, 8, TILE), F32),
            pltpu.VMEM((DEGREE, tiles, rows, TILE), F32),
            pltpu.VMEM((DEGREE, tiles, rows, TILE), F32),
            pltpu.VMEM((2, 1, TILE), F32),
            pltpu.VMEM((2, n_space, 1, TILE), F32),
            pltpu.VMEM((tiles, rows, TILE), F32),
            dma((DEGREE,)),
            dma((DEGREE,)),
            dma((DEGREE,)),
            dma((DEGREE,)),
            dma((DEGREE,)),
            dma((DEGREE,)),
            dma((DEGREE,)),
            dma((DEGREE, n_wave)),
            dma((DEGREE, 2)),
            dma((DEGREE, 2)),
            dma((2,)),
            dma((2,)),
            dma((2,)),
            dma((2,)),
            dma((4 + tiles,)),
        ],
        compiler_params=pltpu.CompilerParams(
            collective_id=0, has_side_effects=True, vmem_limit_bytes=60 * 1024 * 1024
        ),
    )(arranged, positions, wave_index, tile_lists, tile_counts)
    return jnp.transpose(out.reshape(3, vectors, count), (1, 0, 2))


def solution(mesh):
    n_space, n_wave = mesh.shape["space"], mesh.shape["wave"]

    def step(*args):
        return body(n_space, n_wave, *args)

    in_specs = (
        P(None, None, "space"),
        P(None, "space"),
        P(None, "wave"),
        P("space", None),
        P("space"),
    )
    out_specs = P(None, None, "space")
    return jax.shard_map(step, mesh=mesh, in_specs=in_specs, out_specs=out_specs, check_vma=False)
```
